32 devices in a mesh: grp: 2 (over x), ctx: 16 (over z, y, core).
Axes of the slice: x: 2, y: 2, z: 4, core: 2. Of those that a mesh axis runs over, the one named last changes fastest.
Arguments:
- cache_keys: bfloat16 [2048, 512], P(('grp', 'ctx')), parts along dimension 0, may hold values from -4 to 4
- cache_values: bfloat16 [2048, 512], P(('grp', 'ctx')), parts along dimension 0, may hold values from -4 to 4
- new_queries: bfloat16 [2048, 4096], P(('grp', 'ctx')), parts along dimension 0, may hold values from -600 to 600
- new_keys: bfloat16 [2048, 512], P(('grp', 'ctx')), parts along dimension 0, may hold values from -4 to 4
- new_values: bfloat16 [2048, 512], P(('grp', 'ctx')), parts along dimension 0, may hold values from -4 to 4
- cont_queries: bfloat16 [64, 4096], P(('grp', 'ctx')), parts along dimension 0, may hold values from -600 to 600
- suffix_keys: bfloat16 [64, 128, 512], P(('grp', 'ctx')), parts along dimension 0, may hold values from -4 to 4
- suffix_values: bfloat16 [64, 128, 512], P(('grp', 'ctx')), parts along dimension 0, may hold values from -4 to 4
- window_start: int32 [2], P('grp'), parts along dimension 0, may hold values from 0 to 255
- prefix_length: int32 [2], P('grp'), parts along dimension 0, may hold values from 512 to 1024
- suffix_length: int32 [64], P(('grp', 'ctx')), parts along dimension 0, may hold values from 2 to 128
Outputs:
- prompt_out: bfloat16 [2048, 4096], P(('grp', 'ctx')), parts along dimension 0
- cont_out: bfloat16 [64, 4096], P(('grp', 'ctx')), parts along dimension 0
The draws below stay inside these ranges and needn't reach their ends.
There are 2 independent parts, one for each index of `grp`. The reference program is written for one: setup_inputs(seed, part) draws one part's arguments, and reference() takes and returns one part's arrays. A program takes and returns all parts, laid end to end along the dimension named above; each array names one. Nothing has to cross between parts.
All inputs are finite; a program needn't handle non-finite values.
Results may differ from the reference program's by a relative error of at most 0.009.
Values may be sent and summed in bfloat16 or wider, within the bound.
No kernel may reach another device: no remote copies, remote signals or barrier semaphores. Data moves between devices by JAX's collectives and lax.ppermute only.
A program may use at most 192 MiB of HBM per device.

```python
import jax
import jax.numpy as jnp
from jax import lax

H = 32
KVH = 4
HD = 128
GROUP = 8
Q_DEV = 64
C_DEV = 2
SUF = 128
NEW = 1024
WIN = 1024
CONT = 32
N_CTX = 16


def prompt_pair(key):
    folded = jax.random.fold_in(key, 71)
    seed_query, seed_key = jax.random.split(folded, 2)
    queries = jnp.clip(jax.random.normal(seed_query, (NEW, H, HD), jnp.float32), -4.0, 4.0)
    key_rows = jnp.clip(jax.random.normal(seed_key, (NEW, KVH, HD), jnp.float32), -4.0, 4.0)
    return (queries.reshape(NEW, H * HD), key_rows.reshape(NEW, KVH * HD))


def cont_pair(key):
    folded = jax.random.fold_in(key, 83)
    seed_query, seed_key = jax.random.split(folded, 2)
    queries = jnp.clip(jax.random.normal(seed_query, (CONT, H, HD), jnp.float32), -4.0, 4.0)
    suffix_rows = jnp.clip(jax.random.normal(seed_key, (CONT, SUF, KVH, HD), jnp.float32), -4.0, 4.0)
    return (queries.reshape(CONT, H * HD), suffix_rows.reshape(CONT, SUF, KVH * HD))


def draw_new_queries(key, part):
    return prompt_pair(key)[0].astype(jnp.bfloat16)


def draw_new_keys(key, part):
    return prompt_pair(key)[1].astype(jnp.bfloat16)


def draw_cont_queries(key, part):
    return cont_pair(key)[0].astype(jnp.bfloat16)


def draw_suffix_keys(key, part):
    return cont_pair(key)[1].astype(jnp.bfloat16)


def set_ends(entries, key, low, top_value):
    shape = entries.shape
    index_at = [jax.random.randint(jax.random.fold_in(key, axis), (), 0, shape[axis]) for axis in range(len(shape))]
    entries = entries.at[tuple(index_at)].set(low)
    longest = shape.index(max(shape))
    index_at[longest] = (index_at[longest] + 1) % shape[longest]
    return entries.at[tuple(index_at)].set(top_value)


def steps_of(own_key, shape, pieces, smallest, largest):
    loudness = 1.0
    for position, parts in pieces:
        draws = jax.random.uniform(jax.random.fold_in(jax.random.fold_in(own_key, 6), position), (parts,), jnp.float32, smallest / len(pieces), largest / len(pieces))
        loudness = loudness * jnp.repeat(jnp.exp(draws), shape[position] // parts).reshape((-1,) + (1,) * (len(shape) - 1 - position))
    return loudness


def normal_values(own_key, shape, deviation, most, cuts=(), kind=jnp.bfloat16):
    factor_of = steps_of(own_key, shape, cuts, -0.22, 0.18) if cuts else 1.0
    values = jax.random.normal(own_key, shape, jnp.float32) * deviation * factor_of
    return jnp.minimum(jnp.maximum(values, -most), most).astype(kind)


def setup_inputs(seed: int = 0, part: int = 0) -> dict:
    seeds = jax.random.split(jax.random.key(seed), 12)
    part_splits = jax.random.split(jax.random.fold_in(seeds[11], part), 12)
    cache_keys = normal_values(part_splits[0], (WIN, KVH * HD), 1.0, 4.0, ((0, 16),))
    cache_values = normal_values(part_splits[1], (WIN, KVH * HD), 1.0, 4.0, ((0, 16),))
    new_queries = draw_new_queries(jax.random.fold_in(jax.random.fold_in(seeds[11], part), 71), part)
    new_keys = draw_new_keys(jax.random.fold_in(jax.random.fold_in(seeds[11], part), 71), part)
    new_values = normal_values(part_splits[4], (NEW, KVH * HD), 1.0, 4.0, ((0, 16),))
    cont_queries = draw_cont_queries(jax.random.fold_in(jax.random.fold_in(seeds[11], part), 71), part)
    suffix_keys = draw_suffix_keys(jax.random.fold_in(jax.random.fold_in(seeds[11], part), 71), part)
    suffix_values = normal_values(part_splits[7], (CONT, SUF, KVH * HD), 1.0, 4.0, ((0, 16),))
    window_start = jax.random.randint(part_splits[8], (1,), 0, WIN // 4).astype(jnp.int32)
    prefix_length = jax.random.randint(part_splits[9], (1,), WIN // 2, WIN + 1).astype(jnp.int32)
    suffix_length = set_ends(jax.random.randint(part_splits[10], (CONT,), 2, SUF + 1), jax.random.fold_in(part_splits[10], 1), 2, SUF).astype(jnp.int32)
    return dict(cache_keys=cache_keys, cache_values=cache_values, new_queries=new_queries, new_keys=new_keys, new_values=new_values, cont_queries=cont_queries, suffix_keys=suffix_keys, suffix_values=suffix_values, window_start=window_start, prefix_length=prefix_length, suffix_length=suffix_length)


def reference(cache_keys, cache_values, new_queries, new_keys, new_values, cont_queries, suffix_keys, suffix_values, window_start, prefix_length, suffix_length):
    score_scale = HD ** -0.5
    total_rows = WIN + NEW
    every_key = jnp.concatenate([cache_keys, new_keys], axis=0).astype(jnp.float32).reshape(total_rows, KVH, HD)
    every_value = jnp.concatenate([cache_values, new_values], axis=0).astype(jnp.float32).reshape(total_rows, KVH, HD)
    key_index = jnp.arange(total_rows, dtype=jnp.int32)
    in_cache = key_index < WIN
    cache_ok = in_cache & (key_index >= window_start[0]) & (key_index < prefix_length[0])
    prompt_index = key_index - WIN

    def prompt_block(block):
        begin_row = (block * Q_DEV).astype(jnp.int32)
        query_rows = lax.dynamic_slice_in_dim(new_queries, begin_row, Q_DEV, 0)
        heads = query_rows.astype(jnp.float32).reshape(Q_DEV, KVH, GROUP, HD)
        query_index = begin_row + jnp.arange(Q_DEV, dtype=jnp.int32)
        visible = cache_ok[None, :] | ((~in_cache)[None, :] & (prompt_index[None, :] <= query_index[:, None]))
        mask = visible[:, None, None, :]
        scores = jnp.einsum('rkgd,lkd->rkgl', heads, every_key) * score_scale
        scores = jnp.where(mask, scores, -1e30)
        row_max = jnp.max(scores, axis=-1, keepdims=True)
        probs = jnp.where(mask, jnp.exp(scores - row_max), 0.0)
        row_sum = jnp.sum(probs, axis=-1)
        rounded = lax.optimization_barrier(probs.astype(jnp.bfloat16)).astype(jnp.float32)
        mixed = jnp.einsum('rkgl,lkd->rkgd', rounded, every_value) / row_sum[..., None]
        return mixed.reshape(Q_DEV, H * HD).astype(jnp.bfloat16)

    prompt_out = lax.map(prompt_block, jnp.arange(N_CTX, dtype=jnp.int32)).reshape(NEW, H * HD)
    prefix_ok = cache_ok | (~in_cache)

    def cont_block(block):
        begin_row = (block * C_DEV).astype(jnp.int32)
        heads = lax.dynamic_slice_in_dim(cont_queries, begin_row, C_DEV, 0).astype(jnp.float32).reshape(C_DEV, KVH, GROUP, HD)
        own_keys = lax.dynamic_slice_in_dim(suffix_keys, begin_row, C_DEV, 0).astype(jnp.float32).reshape(C_DEV, SUF, KVH, HD)
        own_values = lax.dynamic_slice_in_dim(suffix_values, begin_row, C_DEV, 0).astype(jnp.float32).reshape(C_DEV, SUF, KVH, HD)
        lengths = lax.dynamic_slice_in_dim(suffix_length, begin_row, C_DEV, 0)
        prefix_mask = prefix_ok[None, None, None, :]
        suffix_mask = (jnp.arange(SUF, dtype=jnp.int32)[None, :] < lengths[:, None])[:, None, None, :]
        prefix_scores = jnp.einsum('ckgd,lkd->ckgl', heads, every_key) * score_scale
        prefix_scores = jnp.where(prefix_mask, prefix_scores, -1e30)
        suffix_scores = jnp.einsum('ckgd,cskd->ckgs', heads, own_keys) * score_scale
        suffix_scores = jnp.where(suffix_mask, suffix_scores, -1e30)
        row_max = jnp.maximum(jnp.max(prefix_scores, axis=-1), jnp.max(suffix_scores, axis=-1))[..., None]
        prefix_probs = jnp.where(prefix_mask, jnp.exp(prefix_scores - row_max), 0.0)
        suffix_probs = jnp.where(suffix_mask, jnp.exp(suffix_scores - row_max), 0.0)
        row_sum = jnp.sum(prefix_probs, axis=-1) + jnp.sum(suffix_probs, axis=-1)
        prefix_rounded = lax.optimization_barrier(prefix_probs.astype(jnp.bfloat16)).astype(jnp.float32)
        suffix_rounded = lax.optimization_barrier(suffix_probs.astype(jnp.bfloat16)).astype(jnp.float32)
        mixed = jnp.einsum('ckgl,lkd->ckgd', prefix_rounded, every_value) + jnp.einsum('ckgs,cskd->ckgd', suffix_rounded, own_values)
        mixed = mixed / row_sum[..., None]
        return mixed.reshape(C_DEV, H * HD).astype(jnp.bfloat16)

    cont_out = lax.map(cont_block, jnp.arange(N_CTX, dtype=jnp.int32)).reshape(CONT, H * HD)
    return prompt_out, cont_out
```

```python
import functools

import jax
import jax.numpy as jnp
from jax import lax
from jax.experimental import pallas as pl
from jax.experimental.pallas import tpu as pltpu
from jax.sharding import PartitionSpec as P

KVH = 4
HD = 128
GROUP = 8
SCALE = HD ** (-0.5)
MASKED = -1e30
FLOOR = -1e20
FAR = 1 << 29

VMEM = pl.BlockSpec(memory_space=pltpu.VMEM)
SMEM = pl.BlockSpec(memory_space=pltpu.SMEM)


def ring_chip(place, chips):
    return jnp.where(place < chips // 2, 2 * place, 2 * (chips - 1 - place) + 1)


def ring_place(chip, chips):
    return jnp.where(chip % 2 == 0, chip // 2, chips - 1 - chip // 2)


def ring_pairs(size):
    chips = size // 2
    order = list(range(0, chips, 2)) + list(range(chips - 1, 0, -2))
    place = {chip: index for index, chip in enumerate(order)}
    pairs = []
    for device in range(size):
        chip, core = divmod(device, 2)
        step = 1 if core == 0 else -1
        pairs.append((device, 2 * order[(place[chip] + step) % chips] + core))
    return pairs


def block_origin(device, hop, swapped, partner, size):
    chips = size // 2
    chip, core = device // 2, device % 2
    via = 1 - core if swapped else core
    held = 1 - via if partner else via
    place = ring_place(chip, chips) + jnp.where(via == 0, -hop, hop)
    place = lax.rem(place + 2 * chips, chips)
    return 2 * ring_chip(place, chips) + held


def attend(device, origins, blocks, limits, window, cache_rows, prompt_rows, g, q, state):
    row_max, row_sum, total = state
    keys = cache_rows + prompt_rows
    cols = slice(g * HD, (g + 1) * HD)
    lane = lax.broadcasted_iota(jnp.int32, (1, keys), 1)
    first, last = window
    scores = []
    for origin, block in zip(origins, blocks):
        s = lax.dot_general(
            q, block[:keys, cols], (((1,), (1,)), ((), ())), preferred_element_type=jnp.float32
        )
        at = origin * cache_rows + lane
        cached = jnp.where((at >= first) & (at < last), -1, FAR)
        column = jnp.where(lane < cache_rows, cached, origin * prompt_rows + lane - cache_rows)
        scores.append(jnp.where(column <= limits, s, MASKED))
    high = functools.reduce(jnp.maximum, scores)
    new_max = jnp.maximum(row_max, jnp.max(high, axis=1, keepdims=True))
    weights = [jnp.exp((s - new_max) * SCALE) for s in scores]
    scale_old = jnp.exp((row_max - new_max) * SCALE)
    row_sum = row_sum * scale_old + jnp.sum(
        functools.reduce(jnp.add, weights), axis=1, keepdims=True
    )
    p = jnp.concatenate([w.astype(jnp.bfloat16) for w in weights], axis=1)
    v = jnp.concatenate([block[keys:, cols] for block in blocks], axis=0)
    total = total * scale_old + jnp.dot(p, v, preferred_element_type=jnp.float32)
    return new_max, row_sum, total


def row_limits(device, prompt_rows, cont_rows):
    row = lax.broadcasted_iota(jnp.int32, (GROUP * prompt_rows + cont_rows, 1), 0)
    own = device * prompt_rows + lax.rem(row, prompt_rows)
    return jnp.where(row < GROUP * prompt_rows, own, FAR - 1)


def first_kernel(
    size, cache_rows, prompt_rows, cont_count,
    first_ref, last_ref, length_ref, query_ref, cont_ref, suffix_key_ref, suffix_value_ref, *refs
):
    blocks, (q_ref, max_ref, sum_ref, total_ref) = refs[:-4], refs[-4:]
    device = lax.axis_index("ctx")
    window = (first_ref[0], last_ref[0])
    rows = GROUP * prompt_rows
    suffix_rows = suffix_key_ref.shape[1]
    lane = lax.broadcasted_iota(jnp.int32, (1, suffix_rows), 1)
    limits = row_limits(device, prompt_rows, GROUP * cont_count)
    cont = cont_ref[...].astype(jnp.float32)
    for g in range(KVH):
        heads = [slice((g * GROUP + h) * HD, (g * GROUP + h + 1) * HD) for h in range(GROUP)]
        cont_q = jnp.concatenate(
            [cont[c : c + 1, head] for c in range(cont_count) for head in heads], axis=0
        ).astype(jnp.bfloat16)
        q = jnp.concatenate([query_ref[:, head] for head in heads] + [cont_q], axis=0)
        q_ref[g] = q
        cols = slice(g * HD, (g + 1) * HD)
        maxes, sums, totals = [], [], []
        for c in range(cont_count):
            s = lax.dot_general(
                cont_q, suffix_key_ref[c, :, cols], (((1,), (1,)), ((), ())),
                preferred_element_type=jnp.float32,
            )[c * GROUP : (c + 1) * GROUP]
            s = jnp.where(lane < length_ref[c], s, MASKED)
            high = jnp.maximum(jnp.max(s, axis=1, keepdims=True), FLOOR)
            w = jnp.exp((s - high) * SCALE)
            maxes.append(high)
            sums.append(jnp.sum(w, axis=1, keepdims=True))
            totals.append(
                jnp.dot(
                    w.astype(jnp.bfloat16), suffix_value_ref[c, :, cols],
                    preferred_element_type=jnp.float32,
                )
            )
        state = (
            jnp.concatenate([jnp.full((rows, 1), FLOOR, jnp.float32)] + maxes, axis=0),
            jnp.concatenate([jnp.zeros((rows, 1), jnp.float32)] + sums, axis=0),
            jnp.concatenate([jnp.zeros((rows, HD), jnp.float32)] + totals, axis=0),
        )
        origins = [block_origin(device, 0, False, partner, size) for partner in (False, True)]
        state = attend(
            device, origins, blocks, limits, window, cache_rows, prompt_rows, g, q, state
        )
        max_ref[g] = jnp.broadcast_to(state[0], max_ref.shape[1:])
        sum_ref[g] = jnp.broadcast_to(state[1], sum_ref.shape[1:])
        total_ref[g] = state[2]


def step_kernel(
    size, cache_rows, prompt_rows, cont_count, sources, last_step,
    first_ref, last_ref, q_ref, max_in, sum_in, total_in, *refs
):
    outs = 2 if last_step else 3
    blocks, outs = refs[:-outs], refs[-outs:]
    device = lax.axis_index("ctx")
    window = (first_ref[0], last_ref[0])
    rows = GROUP * prompt_rows
    limits = row_limits(device, prompt_rows, GROUP * cont_count)
    origins = [block_origin(device, *source, size) for source in sources]
    for g in range(KVH):
        state = (max_in[g][:, :1], sum_in[g][:, :1], total_in[g])
        state = attend(
            device, origins, blocks, limits, window, cache_rows, prompt_rows, g, q_ref[g], state
        )
        if not last_step:
            outs[0][g] = jnp.broadcast_to(state[0], outs[0].shape[1:])
            outs[1][g] = jnp.broadcast_to(state[1], outs[1].shape[1:])
            outs[2][g] = state[2]
            continue
        result = state[2] / state[1]
        for h in range(GROUP):
            cols = slice((g * GROUP + h) * HD, (g * GROUP + h + 1) * HD)
            piece = result[h * prompt_rows : (h + 1) * prompt_rows]
            outs[0][:, cols] = piece.astype(jnp.bfloat16)
            rest = [result[rows + c * GROUP + h :][:1] for c in range(cont_count)]
            outs[1][:, cols] = jnp.concatenate(rest, axis=0).astype(jnp.bfloat16)


def cost(rows, keys):
    work = KVH * rows * keys
    return pl.CostEstimate(flops=4 * work * HD, transcendentals=work, bytes_accessed=4 << 20)


def body(
    size,
    cache_keys,
    cache_values,
    new_queries,
    new_keys,
    new_values,
    cont_queries,
    suffix_keys,
    suffix_values,
    window_start,
    prefix_length,
    suffix_length,
):
    cache_rows, prompt_rows, cont_count = (
        cache_keys.shape[0], new_keys.shape[0], cont_queries.shape[0],
    )
    chips = size // 2
    ring = ring_pairs(size)
    pair = [(device, device ^ 1) for device in range(size)]
    send = lambda block, pairs: lax.ppermute(block, "ctx", pairs)

    own = jnp.concatenate([cache_keys, new_keys, cache_values, new_values], axis=0)
    other = send(own, pair)
    rows = GROUP * (prompt_rows + cont_count)
    keys = cache_rows + prompt_rows
    params = pltpu.CompilerParams(vmem_limit_bytes=24 << 20)
    state_shape = [
        jax.ShapeDtypeStruct((KVH, rows, HD), jnp.float32),
        jax.ShapeDtypeStruct((KVH, rows, HD), jnp.float32),
        jax.ShapeDtypeStruct((KVH, rows, HD), jnp.float32),
    ]
    sizes = (size, cache_rows, prompt_rows, cont_count)
    queries, *state = pl.pallas_call(
        functools.partial(first_kernel, *sizes),
        out_shape=[jax.ShapeDtypeStruct((KVH, rows, HD), jnp.bfloat16)] + state_shape,
        in_specs=[SMEM] * 3 + [VMEM] * 6,
        out_specs=[VMEM] * 4,
        compiler_params=params,
        cost_estimate=cost(rows, 3 * keys),
    )(
        window_start, prefix_length, suffix_length, new_queries, cont_queries,
        suffix_keys, suffix_values, own, other,
    )

    def step(state, sources, blocks, last_step=False):
        outs = (
            [jax.ShapeDtypeStruct(new_queries.shape, jnp.bfloat16),
             jax.ShapeDtypeStruct(cont_queries.shape, jnp.bfloat16)]
            if last_step else state_shape
        )
        return pl.pallas_call(
            functools.partial(step_kernel, *sizes, sources, last_step),
            out_shape=outs,
            in_specs=[SMEM] * 2 + [VMEM] * (4 + len(blocks)),
            out_specs=[VMEM] * len(outs),
            input_output_aliases={} if last_step else {3: 0, 4: 1, 5: 2},
            compiler_params=params,
            cost_estimate=cost(rows, len(blocks) * keys),
        )(window_start, prefix_length, queries, *state, *blocks)

    for hop in range(1, chips // 2):
        own, other = send(own, ring), send(other, ring)
        blocks = [own, other, send(own, pair), send(other, pair)]
        sources = [(hop, False, False), (hop, False, True), (hop, True, False), (hop, True, True)]
        state = step(state, sources, blocks)
    own = send(own, ring)
    hop = chips // 2
    sources = [(hop, False, False), (hop, True, False)]
    return tuple(step(state, sources, [own, send(own, pair)], last_step=True))


def solution(mesh):
    in_specs = (
        P(("grp", "ctx"), None),
        P(("grp", "ctx"), None),
        P(("grp", "ctx"), None),
        P(("grp", "ctx"), None),
        P(("grp", "ctx"), None),
        P(("grp", "ctx"), None),
        P(("grp", "ctx"), None, None),
        P(("grp", "ctx"), None, None),
        P("grp"),
        P("grp"),
        P(("grp", "ctx")),
    )
    out_specs = (P(("grp", "ctx"), None), P(("grp", "ctx"), None))
    run = functools.partial(body, mesh.shape["ctx"])
    return jax.shard_map(run, mesh=mesh, in_specs=in_specs, out_specs=out_specs, check_vma=False)
```

```python
import functools
import math

import jax
import jax.numpy as jnp
from jax import lax
from jax.experimental import pallas as pl
from jax.experimental.pallas import tpu as pltpu
from jax.sharding import PartitionSpec as P

KVH = 4
HD = 128
GROUP = 8
SCALE = HD ** (-0.5) * math.log2(math.e)
MASKED = -1e30
FLOOR = -1e20
ONES = 16

VMEM = pl.BlockSpec(memory_space=pltpu.VMEM)
SMEM = pl.BlockSpec(memory_space=pltpu.SMEM)
HBM = pl.BlockSpec(memory_space=pltpu.HBM)
BF16 = jnp.bfloat16
F32 = jnp.float32


def ring_chip(place, chips):
    return jnp.where(place < chips // 2, 2 * place, 2 * (chips - 1 - place) + 1)


def ring_place(chip, chips):
    return jnp.where(chip % 2 == 0, chip // 2, chips - 1 - chip // 2)


def ring_pairs(size):
    chips = size // 2
    order = list(range(0, chips, 2)) + list(range(chips - 1, 0, -2))
    place = {chip: index for index, chip in enumerate(order)}
    pairs = []
    for device in range(size):
        chip, core = divmod(device, 2)
        step = 1 if core == 0 else -1
        pairs.append((device, 2 * order[(place[chip] + step) % chips] + core))
    return pairs


def block_origin(device, hop, swapped, partner, size):
    chips = size // 2
    chip, core = device // 2, device % 2
    via = 1 - core if swapped else core
    held = 1 - via if partner else via
    place = ring_place(chip, chips) + jnp.where(via == 0, -hop, hop)
    place = lax.rem(place + 2 * chips, chips)
    return 2 * ring_chip(place, chips) + held


def pack_kernel(ck_ref, nk_ref, cv_ref, nv_ref, out_ref, value_ref, sems):
    cache_rows, keys = ck_ref.shape[0], value_ref.shape[0]
    copies = [
        pltpu.make_async_copy(source, target, sems.at[index])
        for index, (source, target) in enumerate(
            [
                (cv_ref, value_ref.at[:cache_rows]),
                (nv_ref, value_ref.at[cache_rows:]),
                (ck_ref, out_ref.at[:cache_rows]),
                (nk_ref, out_ref.at[cache_rows:keys]),
            ]
        )
    ]
    for copy in copies:
        copy.start()
    for copy in copies[:2]:
        copy.wait()
    for g in range(KVH):
        out_ref[keys:, g * keys : (g + 1) * keys] = value_ref[:, g * HD : (g + 1) * HD].T
    for copy in copies[2:]:
        copy.wait()


def mask_columns(device, origin, window, cache_rows, prompt_rows):
    keys = cache_rows + prompt_rows
    key = lax.broadcasted_iota(jnp.int32, (keys, HD), 0)
    feature = lax.broadcasted_iota(jnp.int32, (keys, HD), 1)
    first, last = window
    at = origin * cache_rows + key
    outside = (key < cache_rows) & ((at < first) | (at >= last)) & (feature == prompt_rows)
    reach = jnp.where(origin == device, 0, jnp.where(origin < device, -keys, keys + HD))
    late = (key >= cache_rows) & (feature < prompt_rows) & (key - cache_rows + reach > feature)
    return jnp.where(outside | late, MASKED, 0.0).astype(BF16)


def row_features(rows, prompt_rows):
    feature = lax.broadcasted_iota(jnp.int32, (HD, rows), 0)
    row = lax.rem(lax.broadcasted_iota(jnp.int32, (HD, rows), 1), prompt_rows)
    return jnp.where((feature == row) | (feature == prompt_rows), 1.0, 0.0).astype(BF16)


def own_head(full, cont_rows):
    group = lax.broadcasted_iota(jnp.int32, (HD, KVH * cont_rows), 1) // cont_rows
    parts = [jnp.where(group == g, full[g * HD : (g + 1) * HD], 0.0) for g in range(KVH)]
    return jnp.concatenate([functools.reduce(jnp.add, parts), full[KVH * HD :]], axis=0)


def prep_kernel(
    length_ref, query_hbm, cont_hbm, key_hbm, value_hbm,
    q_ref, cont_q_ref, cont_max_ref, cont_total_ref,
    query_ref, cont_ref, key_ref, value_ref, sems,
):
    copies = [
        pltpu.make_async_copy(source, target, sems.at[index])
        for index, (source, target) in enumerate(
            [(query_hbm, query_ref), (cont_hbm, cont_ref), (key_hbm, key_ref), (value_hbm, value_ref)]
        )
    ]
    for copy in copies:
        copy.start()
    prompt_rows = query_ref.shape[0]
    cont_count, suffix_rows = key_ref.shape[:2]
    cont_rows = cont_count * GROUP
    for copy in copies[:2]:
        copy.wait()
    cont = cont_ref[...].astype(F32)
    zeros = jnp.zeros((HD, KVH * cont_rows), F32)
    column = lax.broadcasted_iota(jnp.int32, zeros.shape, 1) // cont_rows
    pieces = []
    for g in range(KVH):
        heads = [slice((g * GROUP + h) * HD, (g * GROUP + h + 1) * HD) for h in range(GROUP)]
        q = jnp.concatenate([query_ref[:, head] for head in heads], axis=0)
        q_ref[g * HD : (g + 1) * HD] = q.T
        pieces += [cont[c : c + 1, head] for c in range(cont_count) for head in heads]
    q_ref[KVH * HD :] = row_features(GROUP * prompt_rows, prompt_rows)
    cont_q = jnp.concatenate(pieces, axis=0).T
    cont_q = jnp.concatenate([jnp.where(column == g, cont_q, 0.0) for g in range(KVH)], axis=0)
    cont_q = cont_q.astype(BF16)
    cont_q_ref[...] = cont_q
    for copy in copies[2:]:
        copy.wait()
    scores = []
    for c in range(cont_count):
        s = jnp.dot(key_ref[c], cont_q, preferred_element_type=F32)
        key = lax.broadcasted_iota(jnp.int32, s.shape, 0)
        owner = lax.broadcasted_iota(jnp.int32, s.shape, 1) % cont_rows // GROUP
        scores.append(jnp.where((owner == c) & (key < length_ref[c]), s, MASKED))
    s = jnp.concatenate(scores, axis=0)
    high = jnp.maximum(jnp.max(s, axis=0, keepdims=True), FLOOR)
    p = jnp.exp2((s - high) * SCALE).astype(BF16)
    v = value_ref[...].reshape(cont_count * suffix_rows, KVH * HD)
    v = jnp.concatenate([v.T, jnp.ones((ONES, v.shape[0]), BF16)], axis=0)
    cont_max_ref[...] = high
    cont_total_ref[...] = own_head(jnp.dot(v, p, preferred_element_type=F32), cont_rows)


def step_kernel(size, cache_rows, prompt_rows, sources, first_step, last_step, *refs):
    first_ref, last_ref, q_ref, cont_q_ref = refs[:4]
    held, refs = (refs[4:6], refs[6:]) if first_step else (refs[4:8], refs[8:])
    blocks, outs = refs[: len(sources)], refs[len(sources) :]
    device = lax.axis_index("ctx")
    window = (first_ref[0], last_ref[0])
    keys = cache_rows + prompt_rows
    rows = GROUP * prompt_rows
    cont_rows = cont_q_ref.shape[1] // KVH
    masks = jnp.concatenate(
        [
            mask_columns(device, block_origin(device, *source, size), window, cache_rows, prompt_rows)
            for source in sources
        ],
        axis=0,
    )
    ones = jnp.ones((ONES, len(blocks) * keys), BF16)

    def merge(scores, old_max, old_total, values):
        new_max = jnp.maximum(old_max, jnp.max(scores, axis=0, keepdims=True))
        p = jnp.exp2((scores - new_max) * SCALE).astype(BF16)
        total = values(p)
        if old_total is not None:
            total = total + old_total * jnp.exp2((old_max - new_max) * SCALE)
        return new_max, total

    values = []
    for g in range(KVH):
        cols = slice(g * HD, (g + 1) * HD)
        k = jnp.concatenate([block[:keys, cols] for block in blocks], axis=0)
        v = jnp.concatenate([block[keys:, g * keys : (g + 1) * keys] for block in blocks], axis=1)
        values.append(v)
        v = jnp.concatenate([v, ones], axis=0)
        s = jnp.dot(
            jnp.concatenate([k, masks], axis=1),
            jnp.concatenate([q_ref[cols], q_ref[KVH * HD :]], axis=0),
            preferred_element_type=F32,
        )
        old = (jnp.full((1, rows), FLOOR, F32), None) if first_step else (held[2][g], held[3][g])
        new_max, total = merge(s, *old, lambda p: jnp.dot(v, p, preferred_element_type=F32))
        if not last_step:
            outs[2][g] = new_max
            outs[3][g] = total
            continue
        result = (total[:HD] * (1.0 / total[HD : HD + 1])).T.astype(BF16)
        for h in range(GROUP):
            cols = slice((g * GROUP + h) * HD, (g * GROUP + h + 1) * HD)
            outs[0][:, cols] = result[h * prompt_rows : (h + 1) * prompt_rows]

    s = sum(
        jnp.dot(
            jnp.concatenate([block[:keys, half * 2 * HD : (half + 1) * 2 * HD] for block in blocks], axis=0),
            cont_q_ref[half * 2 * HD : (half + 1) * 2 * HD],
            preferred_element_type=F32,
        )
        for half in range(KVH // 2)
    )
    hidden = masks[:, prompt_rows : prompt_rows + 1].astype(F32)
    v = jnp.concatenate(values + [ones], axis=0)
    new_max, total = merge(
        s + hidden, held[0][...], held[1][...],
        lambda p: own_head(jnp.dot(v, p, preferred_element_type=F32), cont_rows),
    )
    if not last_step:
        outs[0][...] = new_max
        outs[1][...] = total
        return
    result = (total[:HD] * (1.0 / total[HD : HD + 1])).T
    for row in range(KVH * cont_rows):
        g, c, h = row // cont_rows, row % cont_rows // GROUP, row % GROUP
        cols = slice((g * GROUP + h) * HD, (g * GROUP + h + 1) * HD)
        outs[1][c : c + 1, cols] = result[row : row + 1].astype(BF16)


def in_hbm(array):
    return pltpu.with_memory_space_constraint(array, pltpu.HBM)


def cost(rows, keys):
    work = rows * keys
    return pl.CostEstimate(flops=8 * work * HD, transcendentals=work, bytes_accessed=1 << 20)


def body(
    size,
    cache_keys,
    cache_values,
    new_queries,
    new_keys,
    new_values,
    cont_queries,
    suffix_keys,
    suffix_values,
    window_start,
    prefix_length,
    suffix_length,
):
    cache_rows, prompt_rows, cont_count = (
        cache_keys.shape[0], new_keys.shape[0], cont_queries.shape[0],
    )
    keys = cache_rows + prompt_rows
    chips = size // 2
    ring = ring_pairs(size)
    pair = [(device, device ^ 1) for device in range(size)]
    params = pltpu.CompilerParams(vmem_limit_bytes=24 << 20)
    rows, cont_rows = GROUP * prompt_rows, KVH * GROUP * cont_count
    shape = jax.ShapeDtypeStruct

    def send(block, pairs):
        return lax.ppermute(block, "ctx", pairs)

    own = pl.pallas_call(
        pack_kernel,
        out_shape=shape((keys + HD, KVH * HD), BF16),
        in_specs=[HBM] * 4,
        out_specs=VMEM,
        scratch_shapes=[pltpu.VMEM((keys, KVH * HD), BF16), pltpu.SemaphoreType.DMA((4,))],
        compiler_params=params,
    )(*[in_hbm(x) for x in (cache_keys, new_keys, cache_values, new_values)])
    other = send(own, pair)

    state_shape = [
        shape((1, cont_rows), F32),
        shape((HD + ONES, cont_rows), F32),
        shape((KVH, 1, rows), F32),
        shape((KVH, HD + ONES, rows), F32),
    ]
    queries, cont_q, *state = pl.pallas_call(
        prep_kernel,
        out_shape=[
            shape(((KVH + 1) * HD, rows), BF16),
            shape((KVH * HD, cont_rows), BF16),
        ] + state_shape[:2],
        in_specs=[SMEM] + [HBM] * 4,
        out_specs=[VMEM] * 4,
        scratch_shapes=[
            pltpu.VMEM(new_queries.shape, BF16),
            pltpu.VMEM(cont_queries.shape, BF16),
            pltpu.VMEM(suffix_keys.shape, BF16),
            pltpu.VMEM(suffix_values.shape, BF16),
            pltpu.SemaphoreType.DMA((4,)),
        ],
        compiler_params=params,
        cost_estimate=cost(rows, keys),
    )(suffix_length, *[in_hbm(x) for x in (new_queries, cont_queries, suffix_keys, suffix_values)])

    def step(state, sources, blocks, last_step=False):
        first_step = len(state) == 2
        outs = [shape(new_queries.shape, BF16), shape(cont_queries.shape, BF16)]
        outs = outs if last_step else state_shape
        aliases = {} if last_step else {4 + index: index for index in range(len(state))}
        return pl.pallas_call(
            functools.partial(
                step_kernel, size, cache_rows, prompt_rows, sources, first_step, last_step
            ),
            out_shape=outs,
            in_specs=[SMEM] * 2 + [VMEM] * (2 + len(state) + len(blocks)),
            out_specs=[VMEM] * len(outs),
            input_output_aliases=aliases,
            compiler_params=params,
            cost_estimate=cost(rows, len(blocks) * keys),
        )(window_start, prefix_length, queries, cont_q, *state, *blocks)

    state = step(state, [(0, False, False), (0, False, True)], [own, other])
    for hop in range(1, chips // 2):
        own = send(own, ring)
        other = send(other, ring)
        blocks = [own, other, send(own, pair), send(other, pair)]
        sources = [(hop, False, False), (hop, False, True), (hop, True, False), (hop, True, True)]
        state = step(state, sources, blocks)
    hop = chips // 2
    own = send(own, ring)
    sources = [(hop, False, False), (hop, True, False)]
    blocks = [own, send(own, pair)]
    return tuple(step(state, sources, blocks, last_step=True))


def solution(mesh):
    in_specs = (
        P(("grp", "ctx"), None),
        P(("grp", "ctx"), None),
        P(("grp", "ctx"), None),
        P(("grp", "ctx"), None),
        P(("grp", "ctx"), None),
        P(("grp", "ctx"), None),
        P(("grp", "ctx"), None, None),
        P(("grp", "ctx"), None, None),
        P("grp"),
        P("grp"),
        P(("grp", "ctx")),
    )
    out_specs = (P(("grp", "ctx"), None), P(("grp", "ctx"), None))
    size = mesh.shape["ctx"]

    def run(*arrays):
        return body(size, *arrays)

    return jax.shard_map(run, mesh=mesh, in_specs=in_specs, out_specs=out_specs, check_vma=False)
```

```python
import functools
import math

import jax
import jax.numpy as jnp
from jax import lax
from jax.experimental import pallas as pl
from jax.experimental.pallas import tpu as pltpu
from jax.sharding import PartitionSpec as P

KVH = 4
HD = 128
GROUP = 8
SCALE = HD ** (-0.5) * math.log2(math.e)
MASKED = -1e30
FLOOR = -1e20
ONES = 16

VMEM = pl.BlockSpec(memory_space=pltpu.VMEM)
HBM = pl.BlockSpec(memory_space=pltpu.HBM)
BF16 = jnp.bfloat16
F32 = jnp.float32


def ring_chip(place, chips):
    return jnp.where(place < chips // 2, 2 * place, 2 * (chips - 1 - place) + 1)


def ring_place(chip, chips):
    return jnp.where(chip % 2 == 0, chip // 2, chips - 1 - chip // 2)


def ring_pairs(size):
    chips = size // 2
    order = list(range(0, chips, 2)) + list(range(chips - 1, 0, -2))
    place = {chip: index for index, chip in enumerate(order)}
    pairs = []
    for device in range(size):
        chip, core = divmod(device, 2)
        step = 1 if core == 0 else -1
        pairs.append((device, 2 * order[(place[chip] + step) % chips] + core))
    return pairs


def block_origin(device, hop, swapped, partner, size):
    chips = size // 2
    chip, core = device // 2, device % 2
    via = 1 - core if swapped else core
    held = 1 - via if partner else via
    place = ring_place(chip, chips) + jnp.where(via == 0, -hop, hop)
    place = lax.rem(place + 2 * chips, chips)
    return 2 * ring_chip(place, chips) + held


def pack_kernel(ck_ref, nk_ref, cv_ref, nv_ref, out_ref, value_ref, sems):
    cache_rows, keys = ck_ref.shape[0], value_ref.shape[0]
    copies = [
        pltpu.make_async_copy(source, target, sems.at[index])
        for index, (source, target) in enumerate(
            [
                (cv_ref, value_ref.at[:cache_rows]),
                (nv_ref, value_ref.at[cache_rows:]),
                (ck_ref, out_ref.at[:cache_rows]),
                (nk_ref, out_ref.at[cache_rows:keys]),
            ]
        )
    ]
    for copy in copies:
        copy.start()
    for copy in copies[:2]:
        copy.wait()
    for g in range(KVH):
        out_ref[keys:, g * keys : (g + 1) * keys] = value_ref[:, g * HD : (g + 1) * HD].T
    for copy in copies[2:]:
        copy.wait()


def mask_columns(device, origin, window, cache_rows, prompt_rows, near):
    keys = cache_rows + prompt_rows
    key = lax.broadcasted_iota(jnp.int32, (keys, HD), 0)
    feature = lax.broadcasted_iota(jnp.int32, (keys, HD), 1)
    low = window[0] - origin * cache_rows
    high = jnp.minimum(window[1] - origin * cache_rows, cache_rows)
    top = jnp.where(origin > device, cache_rows, keys)
    cached = (key >= low) & (key < high)
    new = key >= cache_rows
    hidden = jnp.where(cached | new, 0.0, MASKED)
    shown = cached | (new & (key < top))
    masks = jnp.where(shown | (feature != prompt_rows), 0.0, MASKED)
    if near:
        late = (origin == device) & (feature < prompt_rows) & (key - cache_rows > feature)
        masks = jnp.where(late, MASKED, masks)
    return masks.astype(BF16), hidden


def row_features(rows, prompt_rows):
    feature = lax.broadcasted_iota(jnp.int32, (HD, rows), 0)
    row = lax.rem(lax.broadcasted_iota(jnp.int32, (HD, rows), 1), prompt_rows)
    return jnp.where((feature == row) | (feature == prompt_rows), 1.0, 0.0).astype(BF16)


def own_head(full, cont_rows):
    group = lax.broadcasted_iota(jnp.int32, (HD, KVH * cont_rows), 1) // cont_rows
    parts = [jnp.where(group == g, full[g * HD : (g + 1) * HD], 0.0) for g in range(KVH)]
    return jnp.concatenate([functools.reduce(jnp.add, parts), full[KVH * HD :]], axis=0)


def prep_kernel(
    limit_ref, query_hbm, cont_hbm, key_hbm, value_hbm,
    q_ref, cont_q_ref, cont_max_ref, cont_total_ref,
    query_ref, cont_ref, key_ref, value_ref, sems,
):
    copies = [
        pltpu.make_async_copy(source, target, sems.at[index])
        for index, (source, target) in enumerate(
            [
                (query_hbm, query_ref), (cont_hbm, cont_ref), (key_hbm, key_ref), (value_hbm, value_ref),
            ]
        )
    ]
    for copy in copies:
        copy.start()
    prompt_rows = query_ref.shape[0]
    cont_count, suffix_rows = key_ref.shape[:2]
    cont_rows = cont_count * GROUP
    for copy in copies[:2]:
        copy.wait()
    cont = cont_ref[...].astype(F32)
    zeros = jnp.zeros((HD, KVH * cont_rows), F32)
    column = lax.broadcasted_iota(jnp.int32, zeros.shape, 1) // cont_rows
    pieces = []
    for g in range(KVH):
        heads = [slice((g * GROUP + h) * HD, (g * GROUP + h + 1) * HD) for h in range(GROUP)]
        q = jnp.concatenate([query_ref[:, head] for head in heads], axis=0)
        q_ref[g * HD : (g + 1) * HD] = q.T
        pieces += [cont[c : c + 1, head] for c in range(cont_count) for head in heads]
    q_ref[KVH * HD :] = row_features(GROUP * prompt_rows, prompt_rows)
    cont_q = jnp.concatenate(pieces, axis=0).T
    cont_q = jnp.concatenate([jnp.where(column == g, cont_q, 0.0) for g in range(KVH)], axis=0)
    cont_q = cont_q.astype(BF16)
    cont_q_ref[...] = cont_q
    for copy in copies[2:]:
        copy.wait()
    scores = []
    for c in range(cont_count):
        s = jnp.dot(key_ref[c], cont_q, preferred_element_type=F32)
        key = lax.broadcasted_iota(jnp.int32, s.shape, 0)
        owner = lax.broadcasted_iota(jnp.int32, s.shape, 1) % cont_rows // GROUP
        scores.append(jnp.where((owner == c) & (key < limit_ref[2 + c : 3 + c, : KVH * cont_rows]), s, MASKED))
    s = jnp.concatenate(scores, axis=0)
    high = jnp.maximum(jnp.max(s, axis=0, keepdims=True), FLOOR)
    p = jnp.exp2((s - high) * SCALE).astype(BF16)
    v = value_ref[...].reshape(cont_count * suffix_rows, KVH * HD)
    v = jnp.concatenate([v.T, jnp.ones((ONES, v.shape[0]), BF16)], axis=0)
    cont_max_ref[...] = high
    cont_total_ref[...] = own_head(jnp.dot(v, p, preferred_element_type=F32), cont_rows)


def step_kernel(size, cache_rows, prompt_rows, sources, first_step, last_step, *refs):
    limit_ref, q_ref, cont_q_ref = refs[:3]
    held, refs = (refs[3:5], refs[5:]) if first_step else (refs[3:7], refs[7:])
    blocks, outs = refs[: len(sources)], refs[len(sources) :]
    device = lax.axis_index("ctx")
    window = (limit_ref[0:1], limit_ref[1:2])
    keys = cache_rows + prompt_rows
    cont_rows = cont_q_ref.shape[1] // KVH
    pairs = [
        mask_columns(
            device, block_origin(device, *source, size), window, cache_rows, prompt_rows, first_step
        )
        for source in sources
    ]
    masks = jnp.concatenate([pair[0] for pair in pairs], axis=0)
    hidden = jnp.concatenate([pair[1][:, :1] for pair in pairs], axis=0)
    ones = jnp.ones((ONES, len(blocks) * keys), BF16)
    dot = functools.partial(jnp.dot, preferred_element_type=F32)
    values = [
        jnp.concatenate([block[keys:, g * keys : (g + 1) * keys] for block in blocks], axis=1)
        for g in range(KVH)
    ]

    def cont_scores():
        s = sum(
            dot(
                jnp.concatenate([block[:keys, cols] for block in blocks], axis=0), cont_q_ref[cols]
            )
            for cols in (slice(at, at + 2 * HD) for at in range(0, KVH * HD, 2 * HD))
        )
        return s + hidden

    def head_scores(g):
        cols = slice(g * HD, (g + 1) * HD)
        k = jnp.concatenate([block[:keys, cols] for block in blocks], axis=0)
        q = jnp.concatenate([q_ref[cols], q_ref[KVH * HD :]], axis=0)
        return dot(jnp.concatenate([k, masks], axis=1), q)

    def weigh(scores, old_max):
        new_max = jnp.maximum(old_max, jnp.max(scores, axis=0, keepdims=True))
        p = jnp.exp2((scores - new_max) * SCALE).astype(BF16)
        return new_max, p, jnp.exp2((old_max - new_max) * SCALE)

    def finish_cont(s):
        new_max, p, old = weigh(s, held[0][...])
        v = jnp.concatenate(values + [ones], axis=0)
        total = own_head(dot(v, p), cont_rows) + held[1][...] * old
        if not last_step:
            outs[0][...] = new_max
            outs[1][...] = total
            return
        result = (total[:HD] * (1.0 / total[HD : HD + 1])).T
        for row in range(KVH * cont_rows):
            g, c, h = row // cont_rows, row % cont_rows // GROUP, row % GROUP
            cols = slice((g * GROUP + h) * HD, (g * GROUP + h + 1) * HD)
            outs[1][c : c + 1, cols] = result[row : row + 1].astype(BF16)

    def finish_head(g, s):
        new_max, p, old = weigh(s, FLOOR if first_step else held[2][g])
        total = dot(jnp.concatenate([values[g], ones], axis=0), p)
        if not first_step:
            total = total + held[3][g] * old
        if not last_step:
            outs[2][g] = new_max
            outs[3][g] = total
            return
        result = (total[:HD] * (1.0 / total[HD : HD + 1])).T.astype(BF16)
        for h in range(GROUP):
            cols = slice((g * GROUP + h) * HD, (g * GROUP + h + 1) * HD)
            outs[0][:, cols] = result[h * prompt_rows : (h + 1) * prompt_rows]

    work = [(cont_scores, finish_cont)] + [
        (functools.partial(head_scores, g), functools.partial(finish_head, g)) for g in range(KVH)
    ]
    ready = work[0][0]()
    for index, (_, finish) in enumerate(work):
        following = work[index + 1][0]() if index + 1 < len(work) else None
        finish(ready)
        ready = following


def in_hbm(array):
    return pltpu.with_memory_space_constraint(array, pltpu.HBM)


def cost(rows, keys):
    work = rows * keys
    return pl.CostEstimate(flops=8 * work * HD, transcendentals=work, bytes_accessed=1 << 20)


def body(
    size,
    cache_keys,
    cache_values,
    new_queries,
    new_keys,
    new_values,
    cont_queries,
    suffix_keys,
    suffix_values,
    window_start,
    prefix_length,
    suffix_length,
):
    cache_rows, prompt_rows, cont_count = (
        cache_keys.shape[0], new_keys.shape[0], cont_queries.shape[0],
    )
    keys = cache_rows + prompt_rows
    chips = size // 2
    ring = ring_pairs(size)
    pair = [(device, device ^ 1) for device in range(size)]
    params = pltpu.CompilerParams(vmem_limit_bytes=24 << 20)
    rows, cont_rows = GROUP * prompt_rows, KVH * GROUP * cont_count
    shape = jax.ShapeDtypeStruct

    def send(block, pairs):
        return lax.ppermute(block, "ctx", pairs)

    own = pl.pallas_call(
        pack_kernel,
        out_shape=shape((keys + HD, KVH * HD), BF16),
        in_specs=[HBM] * 4,
        out_specs=VMEM,
        scratch_shapes=[pltpu.VMEM((keys, KVH * HD), BF16), pltpu.SemaphoreType.DMA((4,))],
        compiler_params=params,
    )(*[in_hbm(x) for x in (cache_keys, new_keys, cache_values, new_values)])
    other = send(own, pair)

    state_shape = [
        shape((1, cont_rows), F32),
        shape((HD + ONES, cont_rows), F32),
        shape((KVH, 1, rows), F32),
        shape((KVH, HD + ONES, rows), F32),
    ]
    limits = jnp.concatenate([window_start, prefix_length, suffix_length])
    limits = jnp.broadcast_to(limits[:, None], (limits.shape[0], HD))
    queries, cont_q, *state = pl.pallas_call(
        prep_kernel,
        out_shape=[
            shape(((KVH + 1) * HD, rows), BF16),
            shape((KVH * HD, cont_rows), BF16),
        ] + state_shape[:2],
        in_specs=[VMEM] + [HBM] * 4,
        out_specs=[VMEM] * 4,
        scratch_shapes=[
            pltpu.VMEM(new_queries.shape, BF16),
            pltpu.VMEM(cont_queries.shape, BF16),
            pltpu.VMEM(suffix_keys.shape, BF16),
            pltpu.VMEM(suffix_values.shape, BF16),
            pltpu.SemaphoreType.DMA((4,)),
        ],
        compiler_params=params,
        cost_estimate=cost(rows, keys),
    )(limits, *[in_hbm(x) for x in (new_queries, cont_queries, suffix_keys, suffix_values)])

    def take(state, sources, blocks, last_step=False):
        first_step = len(state) == 2
        outs = [shape(new_queries.shape, BF16), shape(cont_queries.shape, BF16)]
        outs = outs if last_step else state_shape
        aliases = {} if last_step else {3 + index: index for index in range(len(state))}
        return pl.pallas_call(
            functools.partial(
                step_kernel, size, cache_rows, prompt_rows, sources, first_step, last_step
            ),
            out_shape=outs,
            in_specs=[VMEM] * (3 + len(state) + len(blocks)),
            out_specs=[VMEM] * len(outs),
            input_output_aliases=aliases,
            compiler_params=params,
            cost_estimate=cost(rows, len(blocks) * keys),
        )(limits, queries, cont_q, *state, *blocks)

    state = take(state, [(0, False, False), (0, False, True)], [own, other])
    hops = chips // 2
    for hop in range(1, hops + 1):
        own = send(own, ring)
        sources = [(hop, False, False), (hop, True, False)]
        blocks = [own, send(own, pair)]
        state = take(state, sources, blocks, last_step=hop == hops)
        if hop < hops:
            other = send(other, ring)
            sources = [(hop, False, True), (hop, True, True)]
            blocks = [other, send(other, pair)]
            state = take(state, sources, blocks)
    return tuple(state)


def solution(mesh):
    in_specs = (
        P(("grp", "ctx"), None),
        P(("grp", "ctx"), None),
        P(("grp", "ctx"), None),
        P(("grp", "ctx"), None),
        P(("grp", "ctx"), None),
        P(("grp", "ctx"), None),
        P(("grp", "ctx"), None, None),
        P(("grp", "ctx"), None, None),
        P("grp"),
        P("grp"),
        P(("grp", "ctx")),
    )
    out_specs = (P(("grp", "ctx"), None), P(("grp", "ctx"), None))
    size = mesh.shape["ctx"]

    def run(*arrays):
        return body(size, *arrays)

    return jax.shard_map(run, mesh=mesh, in_specs=in_specs, out_specs=out_specs, check_vma=False)
```

```python
import functools
import math

import jax
import jax.numpy as jnp
from jax import lax
from jax.experimental import pallas as pl
from jax.experimental.pallas import tpu as pltpu
from jax.sharding import PartitionSpec as P

KVH = 4
HD = 128
GROUP = 8
SCALE = HD ** (-0.5) * math.log2(math.e)
MASKED = -1e30
FLOOR = -1e20
ONES = 16
AHEAD = 3

VMEM = pl.BlockSpec(memory_space=pltpu.VMEM)
SMEM = pl.BlockSpec(memory_space=pltpu.SMEM)
HBM = pl.BlockSpec(memory_space=pltpu.HBM)
BF16 = jnp.bfloat16
F32 = jnp.float32


def ring_chip(place, chips):
    return jnp.where(place < chips // 2, 2 * place, 2 * (chips - 1 - place) + 1)


def ring_place(chip, chips):
    return jnp.where(chip % 2 == 0, chip // 2, chips - 1 - chip // 2)


def ring_pairs(size):
    chips = size // 2
    order = list(range(0, chips, 2)) + list(range(chips - 1, 0, -2))
    place = {chip: index for index, chip in enumerate(order)}
    pairs = []
    for device in range(size):
        chip, core = divmod(device, 2)
        step = 1 if core == 0 else -1
        pairs.append((device, 2 * order[(place[chip] + step) % chips] + core))
    return pairs


def block_origin(device, hop, swapped, partner, size):
    chips = size // 2
    chip, core = device // 2, device % 2
    via = 1 - core if swapped else core
    held = 1 - via if partner else via
    place = ring_place(chip, chips) + jnp.where(via == 0, -hop, hop)
    place = lax.rem(place + 2 * chips, chips)
    return 2 * ring_chip(place, chips) + held


def pack_kernel(ck_hbm, nk_hbm, cv_hbm, nv_hbm, *refs):
    others, out_ref, targets, value_ref, sems = refs[:4], refs[4], refs[5:9], refs[9], refs[10]
    cache_rows, keys = ck_hbm.shape[0], value_ref.shape[0]
    copies = [
        pltpu.make_async_copy(source, target, sems.at[index])
        for index, (source, target) in enumerate(
            [
                (cv_hbm, value_ref.at[:cache_rows]),
                (nv_hbm, value_ref.at[cache_rows:]),
                (ck_hbm, out_ref.at[:cache_rows]),
                (nk_hbm, out_ref.at[cache_rows:keys]),
                *zip(others, targets),
            ]
        )
    ]
    for copy in copies:
        copy.start()
    for copy in copies[:2]:
        copy.wait()
    for g in range(KVH):
        out_ref[keys:, g * keys : (g + 1) * keys] = value_ref[:, g * HD : (g + 1) * HD].T
    for copy in copies[2:]:
        copy.wait()


def mask_columns(device, origin, window, cache_rows, prompt_rows, near):
    keys = cache_rows + prompt_rows
    key = lax.broadcasted_iota(jnp.int32, (keys, HD), 0)
    feature = lax.broadcasted_iota(jnp.int32, (keys, HD), 1)
    low = window[0] - origin * cache_rows
    high = jnp.minimum(window[1] - origin * cache_rows, cache_rows)
    top = jnp.where(origin > device, cache_rows, keys)
    cached = (key >= low) & (key < high)
    new = key >= cache_rows
    hidden = jnp.where(cached | new, 0.0, MASKED)
    shown = cached | (new & (key < top))
    masks = jnp.where(shown | (feature != prompt_rows), 0.0, MASKED)
    if near:
        late = (origin == device) & (feature < prompt_rows) & (key - cache_rows > feature)
        masks = jnp.where(late, MASKED, masks)
    return masks.astype(BF16), hidden


def row_features(rows, prompt_rows):
    feature = lax.broadcasted_iota(jnp.int32, (HD, rows), 0)
    row = lax.rem(lax.broadcasted_iota(jnp.int32, (HD, rows), 1), prompt_rows)
    return jnp.where((feature == row) | (feature == prompt_rows), 1.0, 0.0).astype(BF16)


def own_head(full, cont_rows):
    group = lax.broadcasted_iota(jnp.int32, (HD, KVH * cont_rows), 1) // cont_rows
    parts = [jnp.where(group == g, full[g * HD : (g + 1) * HD], 0.0) for g in range(KVH)]
    return jnp.concatenate([functools.reduce(jnp.add, parts), full[KVH * HD :]], axis=0)


def prep_kernel(
    length_hbm, query_ref, cont_ref, key_ref, value_ref,
    q_ref, cont_q_ref, cont_max_ref, cont_total_ref, length_ref, sem,
):
    load = pltpu.make_async_copy(length_hbm, length_ref, sem)
    load.start()
    prompt_rows = query_ref.shape[0]
    cont_count, suffix_rows = key_ref.shape[:2]
    cont_rows = cont_count * GROUP
    dot = functools.partial(jnp.dot, preferred_element_type=F32)
    cont = cont_ref[...].astype(F32)
    heads = [slice(head * HD, (head + 1) * HD) for head in range(KVH * GROUP)]
    cont_q = jnp.concatenate(
        [
            cont[c : c + 1, head]
            for g in range(KVH)
            for c in range(cont_count)
            for head in heads[g * GROUP : (g + 1) * GROUP]
        ],
        axis=0,
    ).T
    column = lax.broadcasted_iota(jnp.int32, cont_q.shape, 1) // cont_rows
    cont_q = jnp.concatenate([jnp.where(column == g, cont_q, 0.0) for g in range(KVH)], axis=0)
    cont_q = cont_q.astype(BF16)
    cont_q_ref[...] = cont_q
    scores = [dot(key_ref[c], cont_q) for c in range(cont_count)]
    for g in range(KVH):
        q = jnp.concatenate([query_ref[:, head] for head in heads[g * GROUP : (g + 1) * GROUP]], axis=0)
        q_ref[g * HD : (g + 1) * HD] = q.T
    q_ref[KVH * HD :] = row_features(GROUP * prompt_rows, prompt_rows)
    v = value_ref[...].reshape(cont_count * suffix_rows, KVH * HD).T
    v = jnp.concatenate([v, jnp.ones((ONES, v.shape[1]), BF16)], axis=0)
    load.wait()
    key = lax.broadcasted_iota(jnp.int32, scores[0].shape, 0)
    owner = lax.broadcasted_iota(jnp.int32, scores[0].shape, 1) % cont_rows // GROUP
    s = jnp.concatenate(
        [
            jnp.where((owner == c) & (key < length_ref[c]), scores[c], MASKED)
            for c in range(cont_count)
        ],
        axis=0,
    )
    new_max, p, _ = weigh(s, FLOOR)
    cont_max_ref[...] = new_max
    cont_total_ref[...] = own_head(dot(v, p), cont_rows)


def window_kernel(first_ref, last_ref, window_ref):
    window_ref[0:1] = jnp.full((1, HD), first_ref[0], jnp.int32)
    window_ref[1:2] = jnp.full((1, HD), last_ref[0], jnp.int32)


def weigh(scores, old_max):
    new_max = jnp.maximum(old_max, jnp.max(scores, axis=0, keepdims=True))
    p = jnp.exp2((scores - new_max) * SCALE).astype(BF16)
    return new_max, p, jnp.exp2((old_max - new_max) * SCALE)


def take_kernel(size, cache_rows, prompt_rows, cont_count, sources, kind, *refs):
    first, last = kind == "first", kind == "last"
    window_ref, q_ref, cont_q_ref = refs[:3]
    held, refs = (refs[3:5], refs[5:]) if first else (refs[3:7], refs[7:])
    blocks, outs = refs[: len(sources)], refs[len(sources) :]
    device = lax.axis_index("ctx")
    keys = cache_rows + prompt_rows
    cont_rows = cont_count * GROUP
    ones = jnp.ones((ONES, len(blocks) * keys), BF16)
    dot = functools.partial(jnp.dot, preferred_element_type=F32)
    if last:
        out_hbm, cont_hbm, out_ref, cont_ref, sems = outs

    window = (window_ref[0:1], window_ref[1:2])
    terms = [
        mask_columns(
            device, block_origin(device, *source, size), window, cache_rows, prompt_rows, source[0] == 0
        )
        for source in sources
    ]
    masks = jnp.concatenate([term[0] for term in terms], axis=0)
    hidden = jnp.concatenate([term[1][:, :1] for term in terms], axis=0)
    values = [
        jnp.concatenate([block[keys:, g * keys : (g + 1) * keys] for block in blocks], axis=1)
        for g in range(KVH)
    ]
    stores = []

    def cont_scores():
        cuts = [slice(at, at + 2 * HD) for at in range(0, KVH * HD, 2 * HD)]
        parts = [
            dot(jnp.concatenate([block[:keys, cut] for block in blocks], axis=0), cont_q_ref[cut])
            for cut in cuts
        ]
        return sum(parts) + hidden

    def finish_cont(s):
        new_max, p, old = weigh(s, held[0][...])
        total = own_head(dot(jnp.concatenate(values + [ones], axis=0), p), cont_rows)
        total = total + held[1][...] * old
        if not last:
            outs[0][...] = new_max
            outs[1][...] = total
            return
        result = (total[:HD] * (1.0 / total[HD : HD + 1])).T
        for row in range(KVH * cont_rows):
            g, c, h = row // cont_rows, row % cont_rows // GROUP, row % GROUP
            cols = slice((g * GROUP + h) * HD, (g * GROUP + h + 1) * HD)
            cont_ref[c : c + 1, cols] = result[row : row + 1].astype(BF16)
        stores.append(pltpu.make_async_copy(cont_ref, cont_hbm, sems.at[KVH]))
        stores[-1].start()

    def head_scores(g):
        cols = slice(g * HD, (g + 1) * HD)
        k = jnp.concatenate([block[:keys, cols] for block in blocks], axis=0)
        q = jnp.concatenate([q_ref[cols], q_ref[KVH * HD :]], axis=0)
        return dot(jnp.concatenate([k, masks], axis=1), q)

    def finish_head(g, s):
        new_max, p, old = weigh(s, FLOOR if first else held[2][g])
        total = dot(jnp.concatenate([values[g], ones], axis=0), p)
        if not first:
            total = total + held[3][g] * old
        if not last:
            outs[2][g] = new_max
            outs[3][g] = total
            return
        result = (total[:HD] * (1.0 / total[HD : HD + 1])).T.astype(BF16)
        for h in range(GROUP):
            cols = slice((g * GROUP + h) * HD, (g * GROUP + h + 1) * HD)
            out_ref[:, cols] = result[h * prompt_rows : (h + 1) * prompt_rows]
        cols = slice(g * GROUP * HD, (g + 1) * GROUP * HD)
        stores.append(
            pltpu.make_async_copy(out_ref.at[:, cols], out_hbm.at[:, cols], sems.at[g])
        )
        stores[-1].start()

    work = [(cont_scores, finish_cont)] + [
        (functools.partial(head_scores, g), functools.partial(finish_head, g)) for g in range(KVH)
    ]
    ready = [scores() for scores, _ in work[:AHEAD]]
    for index, (_, finish) in enumerate(work):
        if index + AHEAD < len(work):
            ready.append(work[index + AHEAD][0]())
        finish(ready[index])
    for store in stores:
        store.wait()


def in_hbm(array):
    return pltpu.with_memory_space_constraint(array, pltpu.HBM)


def cost(rows, keys):
    work = rows * keys
    return pl.CostEstimate(flops=8 * work * HD, transcendentals=work, bytes_accessed=1 << 20)


def body(
    size,
    cache_keys,
    cache_values,
    new_queries,
    new_keys,
    new_values,
    cont_queries,
    suffix_keys,
    suffix_values,
    window_start,
    prefix_length,
    suffix_length,
):
    cache_rows, prompt_rows, cont_count = (
        cache_keys.shape[0], new_keys.shape[0], cont_queries.shape[0],
    )
    keys = cache_rows + prompt_rows
    chips = size // 2
    ring = ring_pairs(size)
    pair = [(device, device ^ 1) for device in range(size)]
    params = pltpu.CompilerParams(vmem_limit_bytes=24 << 20)
    rows, cont_rows = GROUP * prompt_rows, KVH * GROUP * cont_count
    shape = jax.ShapeDtypeStruct

    def send(block, pairs):
        return lax.ppermute(block, "ctx", pairs)

    rest = (new_queries, cont_queries, suffix_keys, suffix_values)
    arrays = (cache_keys, new_keys, cache_values, new_values, *rest)
    own, *rest = pl.pallas_call(
        pack_kernel,
        out_shape=[shape((keys + HD, KVH * HD), BF16)] + [shape(x.shape, BF16) for x in rest],
        in_specs=[HBM] * 8,
        out_specs=[VMEM] * 5,
        scratch_shapes=[pltpu.VMEM((keys, KVH * HD), BF16), pltpu.SemaphoreType.DMA((8,))],
        compiler_params=params,
    )(*[in_hbm(x) for x in arrays])
    other = send(own, pair)
    waiting = [((0, False, False), own), ((0, False, True), other)]

    state_shape = [
        shape((1, cont_rows), F32),
        shape((HD + ONES, cont_rows), F32),
        shape((KVH, 1, rows), F32),
        shape((KVH, HD + ONES, rows), F32),
    ]
    queries, cont_q, *state = pl.pallas_call(
        prep_kernel,
        out_shape=[
            shape(((KVH + 1) * HD, rows), BF16),
            shape((KVH * HD, cont_rows), BF16),
        ] + state_shape[:2],
        in_specs=[HBM] + [VMEM] * 4,
        out_specs=[VMEM] * 4,
        scratch_shapes=[pltpu.SMEM(suffix_length.shape, jnp.int32), pltpu.SemaphoreType.DMA(())],
        compiler_params=params,
        cost_estimate=cost(rows, keys),
    )(in_hbm(suffix_length), *rest)

    window = pl.pallas_call(
        window_kernel,
        out_shape=shape((2, HD), jnp.int32),
        in_specs=[SMEM] * 2,
        out_specs=VMEM,
        compiler_params=params,
    )(window_start, prefix_length)

    def take(state, held, kind="middle"):
        sources, blocks = zip(*held)
        specs, scratch, outs = [VMEM] * 4, [], state_shape
        if kind == "last":
            outs = [shape(new_queries.shape, BF16), shape(cont_queries.shape, BF16)]
            specs = [HBM] * 2
            scratch = [
                pltpu.VMEM(new_queries.shape, BF16),
                pltpu.VMEM(cont_queries.shape, BF16),
                pltpu.SemaphoreType.DMA((KVH + 1,)),
            ]
        aliases = {} if kind == "last" else {3 + index: index for index in range(len(state))}
        return pl.pallas_call(
            functools.partial(
                take_kernel, size, cache_rows, prompt_rows, cont_count, sources, kind
            ),
            out_shape=outs,
            in_specs=[VMEM] * (3 + len(state) + len(blocks)),
            out_specs=specs,
            scratch_shapes=scratch,
            input_output_aliases=aliases,
            compiler_params=params,
            cost_estimate=cost(rows, len(blocks) * keys),
        )(window, queries, cont_q, *state, *blocks)

    hops = chips // 2
    for hop in range(1, hops):
        own, other = send(own, ring), send(other, ring)
        swap, swop = send(own, pair), send(other, pair)
        arrived = [((hop, False, False), own), ((hop, True, False), swap)]
        if hop == 1:
            state = take(state, waiting, "first")
            waiting = []
        else:
            state = take(state, waiting[:2])
            waiting = waiting[2:]
            if hop + 1 == hops:
                waiting, arrived = waiting + arrived, []
            state = take(state, waiting)
            waiting = []
        waiting += arrived + [((hop, False, True), other), ((hop, True, True), swop)]
    own = send(own, ring)
    swapped = send(own, pair)
    state = take(state, waiting + [((hops, False, False), own)])
    return tuple(take(state, [((hops, True, False), swapped)], "last"))


def solution(mesh):
    in_specs = (
        P(("grp", "ctx"), None),
        P(("grp", "ctx"), None),
        P(("grp", "ctx"), None),
        P(("grp", "ctx"), None),
        P(("grp", "ctx"), None),
        P(("grp", "ctx"), None),
        P(("grp", "ctx"), None, None),
        P(("grp", "ctx"), None, None),
        P("grp"),
        P("grp"),
        P(("grp", "ctx")),
    )
    out_specs = (P(("grp", "ctx"), None), P(("grp", "ctx"), None))
    size = mesh.shape["ctx"]

    def run(*arrays):
        return body(size, *arrays)

    return jax.shard_map(run, mesh=mesh, in_specs=in_specs, out_specs=out_specs, check_vma=False)
```

```python
import functools
import math

import jax
import jax.numpy as jnp
from jax import lax
from jax.experimental import pallas as pl
from jax.experimental.pallas import tpu as pltpu
from jax.sharding import PartitionSpec as P

KVH = 4
HD = 128
GROUP = 8
SCALE = HD ** (-0.5) * math.log2(math.e)
MASKED = -1e30
FLOOR = -1e20
ONES = 16
AHEAD = 3

VMEM = pl.BlockSpec(memory_space=pltpu.VMEM)
SMEM = pl.BlockSpec(memory_space=pltpu.SMEM)
HBM = pl.BlockSpec(memory_space=pltpu.HBM)
BF16 = jnp.bfloat16
F32 = jnp.float32


def ring_chip(place, chips):
    return jnp.where(place < chips // 2, 2 * place, 2 * (chips - 1 - place) + 1)


def ring_place(chip, chips):
    return jnp.where(chip % 2 == 0, chip // 2, chips - 1 - chip // 2)


def ring_pairs(size):
    chips = size // 2
    order = list(range(0, chips, 2)) + list(range(chips - 1, 0, -2))
    pairs = []
    for place, chip in enumerate(order):
        for way, step in enumerate((1, -1)):
            core = (place + way) % 2
            pairs.append((2 * chip + core, 2 * order[(place + step) % chips] + 1 - core))
    return sorted(pairs)


def block_origin(device, hop, swapped, partner, size):
    chips = size // 2
    chip, core = device // 2, device % 2
    place = ring_place(chip, chips)
    way = (core + place) % 2
    if swapped:
        way = 1 - way
    place = lax.rem(place + jnp.where(way == 0, -hop, hop) + 2 * chips, chips)
    held = (way + place) % 2
    if partner:
        held = 1 - held
    return 2 * ring_chip(place, chips) + held


def pack_kernel(ck_hbm, nk_hbm, cv_hbm, nv_hbm, *refs):
    others, out_ref, targets, value_ref, sems = refs[:4], refs[4], refs[5:9], refs[9], refs[10]
    cache_rows, keys = ck_hbm.shape[0], value_ref.shape[0]
    copies = [
        pltpu.make_async_copy(source, target, sems.at[index])
        for index, (source, target) in enumerate(
            [
                (cv_hbm, value_ref.at[:cache_rows]),
                (nv_hbm, value_ref.at[cache_rows:]),
                (ck_hbm, out_ref.at[:cache_rows]),
                (nk_hbm, out_ref.at[cache_rows:keys]),
                *zip(others, targets),
            ]
        )
    ]
    for copy in copies:
        copy.start()
    for copy in copies[:2]:
        copy.wait()
    for g in range(KVH):
        out_ref[keys:, g * keys : (g + 1) * keys] = value_ref[:, g * HD : (g + 1) * HD].T
    for copy in copies[2:]:
        copy.wait()


def mask_columns(device, origin, window, cache_rows, prompt_rows, near):
    keys = cache_rows + prompt_rows
    key = lax.broadcasted_iota(jnp.int32, (keys, HD), 0)
    feature = lax.broadcasted_iota(jnp.int32, (keys, HD), 1)
    low = window[0] - origin * cache_rows
    high = jnp.minimum(window[1] - origin * cache_rows, cache_rows)
    top = jnp.where(origin > device, cache_rows, keys)
    cached = (key >= low) & (key < high)
    new = key >= cache_rows
    hidden = jnp.where(cached | new, 0.0, MASKED)
    shown = cached | (new & (key < top))
    masks = jnp.where(shown | (feature != prompt_rows), 0.0, MASKED)
    if near:
        late = (origin == device) & (feature < prompt_rows) & (key - cache_rows > feature)
        masks = jnp.where(late, MASKED, masks)
    return masks.astype(BF16), hidden


def row_features(rows, prompt_rows):
    feature = lax.broadcasted_iota(jnp.int32, (HD, rows), 0)
    row = lax.rem(lax.broadcasted_iota(jnp.int32, (HD, rows), 1), prompt_rows)
    return jnp.where((feature == row) | (feature == prompt_rows), 1.0, 0.0).astype(BF16)


def own_head(full, cont_rows):
    group = lax.broadcasted_iota(jnp.int32, (HD, KVH * cont_rows), 1) // cont_rows
    parts = [jnp.where(group == g, full[g * HD : (g + 1) * HD], 0.0) for g in range(KVH)]
    return jnp.concatenate([functools.reduce(jnp.add, parts), full[KVH * HD :]], axis=0)


def prep_kernel(
    length_hbm, query_ref, cont_ref, key_ref, value_ref,
    q_ref, cont_q_ref, cont_max_ref, cont_total_ref, length_ref, sem,
):
    load = pltpu.make_async_copy(length_hbm, length_ref, sem)
    load.start()
    prompt_rows = query_ref.shape[0]
    cont_count, suffix_rows = key_ref.shape[:2]
    cont_rows = cont_count * GROUP
    dot = functools.partial(jnp.dot, preferred_element_type=F32)
    cont = cont_ref[...].astype(F32)
    heads = [slice(head * HD, (head + 1) * HD) for head in range(KVH * GROUP)]
    cont_q = jnp.concatenate(
        [
            cont[c : c + 1, head]
            for g in range(KVH)
            for c in range(cont_count)
            for head in heads[g * GROUP : (g + 1) * GROUP]
        ],
        axis=0,
    ).T
    column = lax.broadcasted_iota(jnp.int32, cont_q.shape, 1) // cont_rows
    cont_q = jnp.concatenate([jnp.where(column == g, cont_q, 0.0) for g in range(KVH)], axis=0)
    cont_q = cont_q.astype(BF16)
    cont_q_ref[...] = cont_q
    scores = [dot(key_ref[c], cont_q) for c in range(cont_count)]
    for g in range(KVH):
        q = jnp.concatenate([query_ref[:, head] for head in heads[g * GROUP : (g + 1) * GROUP]], axis=0)
        q_ref[g * HD : (g + 1) * HD] = q.T
    q_ref[KVH * HD :] = row_features(GROUP * prompt_rows, prompt_rows)
    v = value_ref[...].reshape(cont_count * suffix_rows, KVH * HD).T
    v = jnp.concatenate([v, jnp.ones((ONES, v.shape[1]), BF16)], axis=0)
    load.wait()
    key = lax.broadcasted_iota(jnp.int32, scores[0].shape, 0)
    owner = lax.broadcasted_iota(jnp.int32, scores[0].shape, 1) % cont_rows // GROUP
    s = jnp.concatenate(
        [
            jnp.where((owner == c) & (key < length_ref[c]), scores[c], MASKED)
            for c in range(cont_count)
        ],
        axis=0,
    )
    new_max, p, _ = weigh(s, FLOOR)
    cont_max_ref[...] = new_max
    cont_total_ref[...] = own_head(dot(v, p), cont_rows)


def window_kernel(first_ref, last_ref, window_ref):
    window_ref[0:1] = jnp.full((1, HD), first_ref[0], jnp.int32)
    window_ref[1:2] = jnp.full((1, HD), last_ref[0], jnp.int32)


def weigh(scores, old_max):
    new_max = jnp.maximum(old_max, jnp.max(scores, axis=0, keepdims=True))
    p = jnp.exp2((scores - new_max) * SCALE).astype(BF16)
    return new_max, p, jnp.exp2((old_max - new_max) * SCALE)


def take_kernel(size, cache_rows, prompt_rows, cont_count, sources, kind, *refs):
    first, last = kind == "first", kind == "last"
    window_ref, q_ref, cont_q_ref = refs[:3]
    held, refs = (refs[3:5], refs[5:]) if first else (refs[3:7], refs[7:])
    blocks, outs = refs[: len(sources)], refs[len(sources) :]
    device = lax.axis_index("ctx")
    keys = cache_rows + prompt_rows
    cont_rows = cont_count * GROUP
    ones = jnp.ones((ONES, len(blocks) * keys), BF16)
    dot = functools.partial(jnp.dot, preferred_element_type=F32)
    if last:
        out_hbm, cont_hbm, out_ref, cont_ref, sems = outs

    window = (window_ref[0:1], window_ref[1:2])
    terms = [
        mask_columns(
            device, block_origin(device, *source, size), window, cache_rows, prompt_rows, source[0] == 0
        )
        for source in sources
    ]
    masks = jnp.concatenate([term[0] for term in terms], axis=0)
    hidden = jnp.concatenate([term[1][:, :1] for term in terms], axis=0)
    values = [
        jnp.concatenate([block[keys:, g * keys : (g + 1) * keys] for block in blocks], axis=1)
        for g in range(KVH)
    ]
    stores = []

    def cont_scores():
        cuts = [slice(at, at + 2 * HD) for at in range(0, KVH * HD, 2 * HD)]
        parts = [
            dot(jnp.concatenate([block[:keys, cut] for block in blocks], axis=0), cont_q_ref[cut])
            for cut in cuts
        ]
        return sum(parts) + hidden

    def finish_cont(s):
        new_max, p, old = weigh(s, held[0][...])
        total = own_head(dot(jnp.concatenate(values + [ones], axis=0), p), cont_rows)
        total = total + held[1][...] * old
        if not last:
            outs[0][...] = new_max
            outs[1][...] = total
            return
        result = (total[:HD] * (1.0 / total[HD : HD + 1])).T
        for row in range(KVH * cont_rows):
            g, c, h = row // cont_rows, row % cont_rows // GROUP, row % GROUP
            cols = slice((g * GROUP + h) * HD, (g * GROUP + h + 1) * HD)
            cont_ref[c : c + 1, cols] = result[row : row + 1].astype(BF16)
        stores.append(pltpu.make_async_copy(cont_ref, cont_hbm, sems.at[KVH]))
        stores[-1].start()

    def head_scores(g):
        cols = slice(g * HD, (g + 1) * HD)
        k = jnp.concatenate([block[:keys, cols] for block in blocks], axis=0)
        q = jnp.concatenate([q_ref[cols], q_ref[KVH * HD :]], axis=0)
        return dot(jnp.concatenate([k, masks], axis=1), q)

    def finish_head(g, s):
        new_max, p, old = weigh(s, FLOOR if first else held[2][g])
        total = dot(jnp.concatenate([values[g], ones], axis=0), p)
        if not first:
            total = total + held[3][g] * old
        if not last:
            outs[2][g] = new_max
            outs[3][g] = total
            return
        result = (total[:HD] * (1.0 / total[HD : HD + 1])).T.astype(BF16)
        for h in range(GROUP):
            cols = slice((g * GROUP + h) * HD, (g * GROUP + h + 1) * HD)
            out_ref[:, cols] = result[h * prompt_rows : (h + 1) * prompt_rows]
        cols = slice(g * GROUP * HD, (g + 1) * GROUP * HD)
        stores.append(
            pltpu.make_async_copy(out_ref.at[:, cols], out_hbm.at[:, cols], sems.at[g])
        )
        stores[-1].start()

    work = [(cont_scores, finish_cont)] + [
        (functools.partial(head_scores, g), functools.partial(finish_head, g)) for g in range(KVH)
    ]
    ready = [scores() for scores, _ in work[:AHEAD]]
    for index, (_, finish) in enumerate(work):
        if index + AHEAD < len(work):
            ready.append(work[index + AHEAD][0]())
        finish(ready[index])
    for store in stores:
        store.wait()


def in_hbm(array):
    return pltpu.with_memory_space_constraint(array, pltpu.HBM)


def cost(rows, keys):
    work = rows * keys
    return pl.CostEstimate(flops=8 * work * HD, transcendentals=work, bytes_accessed=1 << 20)


def body(
    size,
    cache_keys,
    cache_values,
    new_queries,
    new_keys,
    new_values,
    cont_queries,
    suffix_keys,
    suffix_values,
    window_start,
    prefix_length,
    suffix_length,
):
    cache_rows, prompt_rows, cont_count = (
        cache_keys.shape[0], new_keys.shape[0], cont_queries.shape[0],
    )
    keys = cache_rows + prompt_rows
    chips = size // 2
    ring = ring_pairs(size)
    pair = [(device, device ^ 1) for device in range(size)]
    params = pltpu.CompilerParams(vmem_limit_bytes=24 << 20)
    rows, cont_rows = GROUP * prompt_rows, KVH * GROUP * cont_count
    shape = jax.ShapeDtypeStruct

    def send(block, pairs):
        return lax.ppermute(block, "ctx", pairs)

    rest = (new_queries, cont_queries, suffix_keys, suffix_values)
    arrays = (cache_keys, new_keys, cache_values, new_values, *rest)
    own, *rest = pl.pallas_call(
        pack_kernel,
        out_shape=[shape((keys + HD, KVH * HD), BF16)] + [shape(x.shape, BF16) for x in rest],
        in_specs=[HBM] * 8,
        out_specs=[VMEM] * 5,
        scratch_shapes=[pltpu.VMEM((keys, KVH * HD), BF16), pltpu.SemaphoreType.DMA((8,))],
        compiler_params=params,
    )(*[in_hbm(x) for x in arrays])
    other = send(own, pair)
    waiting = [((0, False, False), own), ((0, False, True), other)]

    state_shape = [
        shape((1, cont_rows), F32),
        shape((HD + ONES, cont_rows), F32),
        shape((KVH, 1, rows), F32),
        shape((KVH, HD + ONES, rows), F32),
    ]
    queries, cont_q, *state = pl.pallas_call(
        prep_kernel,
        out_shape=[
            shape(((KVH + 1) * HD, rows), BF16),
            shape((KVH * HD, cont_rows), BF16),
        ] + state_shape[:2],
        in_specs=[HBM] + [VMEM] * 4,
        out_specs=[VMEM] * 4,
        scratch_shapes=[pltpu.SMEM(suffix_length.shape, jnp.int32), pltpu.SemaphoreType.DMA(())],
        compiler_params=params,
        cost_estimate=cost(rows, keys),
    )(in_hbm(suffix_length), *rest)

    window = pl.pallas_call(
        window_kernel,
        out_shape=shape((2, HD), jnp.int32),
        in_specs=[SMEM] * 2,
        out_specs=VMEM,
        compiler_params=params,
    )(window_start, prefix_length)

    def take(state, held, kind="middle"):
        sources, blocks = zip(*held)
        specs, scratch, outs = [VMEM] * 4, [], state_shape
        if kind == "last":
            outs = [shape(new_queries.shape, BF16), shape(cont_queries.shape, BF16)]
            specs = [HBM] * 2
            scratch = [
                pltpu.VMEM(new_queries.shape, BF16),
                pltpu.VMEM(cont_queries.shape, BF16),
                pltpu.SemaphoreType.DMA((KVH + 1,)),
            ]
        aliases = {} if kind == "last" else {3 + index: index for index in range(len(state))}
        return pl.pallas_call(
            functools.partial(
                take_kernel, size, cache_rows, prompt_rows, cont_count, sources, kind
            ),
            out_shape=outs,
            in_specs=[VMEM] * (3 + len(state) + len(blocks)),
            out_specs=specs,
            scratch_shapes=scratch,
            input_output_aliases=aliases,
            compiler_params=params,
            cost_estimate=cost(rows, len(blocks) * keys),
        )(window, queries, cont_q, *state, *blocks)

    hops = chips // 2
    for hop in range(1, hops):
        own, other = send(own, ring), send(other, ring)
        swap, swop = send(own, pair), send(other, pair)
        arrived = [((hop, False, False), own), ((hop, True, False), swap)]
        if hop == 1:
            state = take(state, waiting, "first")
            waiting = []
        else:
            state = take(state, waiting[:2])
            waiting = waiting[2:]
            if hop + 1 == hops:
                waiting, arrived = waiting + arrived, []
            state = take(state, waiting)
            waiting = []
        waiting += arrived + [((hop, False, True), other), ((hop, True, True), swop)]
    own = send(own, ring)
    swapped = send(own, pair)
    state = take(state, waiting + [((hops, False, False), own)])
    return tuple(take(state, [((hops, True, False), swapped)], "last"))


def solution(mesh):
    in_specs = (
        P(("grp", "ctx"), None),
        P(("grp", "ctx"), None),
        P(("grp", "ctx"), None),
        P(("grp", "ctx"), None),
        P(("grp", "ctx"), None),
        P(("grp", "ctx"), None),
        P(("grp", "ctx"), None, None),
        P(("grp", "ctx"), None, None),
        P("grp"),
        P("grp"),
        P(("grp", "ctx")),
    )
    out_specs = (P(("grp", "ctx"), None), P(("grp", "ctx"), None))
    size = mesh.shape["ctx"]

    def run(*arrays):
        return body(size, *arrays)

    return jax.shard_map(run, mesh=mesh, in_specs=in_specs, out_specs=out_specs, check_vma=False)
```

```python
import functools
import math

import jax
import jax.numpy as jnp
from jax import lax
from jax.experimental import pallas as pl
from jax.experimental.pallas import tpu as pltpu
from jax.sharding import PartitionSpec as P

KVH = 4
HD = 128
GROUP = 8
SCALE = HD ** (-0.5) * math.log2(math.e)
MASKED = -1e30
FLOOR = -1e20
ONES = 16
AHEAD = 3

VMEM = pl.BlockSpec(memory_space=pltpu.VMEM)
SMEM = pl.BlockSpec(memory_space=pltpu.SMEM)
HBM = pl.BlockSpec(memory_space=pltpu.HBM)
BF16 = jnp.bfloat16
F32 = jnp.float32


def ring_chip(place, chips):
    return jnp.where(place < chips // 2, 2 * place, 2 * (chips - 1 - place) + 1)


def ring_place(chip, chips):
    return jnp.where(chip % 2 == 0, chip // 2, chips - 1 - chip // 2)


def ring_pairs(size):
    chips = size // 2
    order = list(range(0, chips, 2)) + list(range(chips - 1, 0, -2))
    pairs = []
    for place, chip in enumerate(order):
        for way, step in enumerate((1, -1)):
            core = (place + way) % 2
            pairs.append((2 * chip + core, 2 * order[(place + step) % chips] + 1 - core))
    return sorted(pairs)


def block_origin(device, hop, swapped, partner, size):
    chips = size // 2
    chip, core = device // 2, device % 2
    place = ring_place(chip, chips)
    way = (core + place) % 2
    if swapped:
        way = 1 - way
    place = lax.rem(place + jnp.where(way == 0, -hop, hop) + 2 * chips, chips)
    held = (way + place) % 2
    if partner:
        held = 1 - held
    return 2 * ring_chip(place, chips) + held


def pack_kernel(ck_hbm, nk_hbm, cv_hbm, nv_hbm, out_ref, value_ref, sems):
    cache_rows, keys = ck_hbm.shape[0], value_ref.shape[0]
    copies = [
        pltpu.make_async_copy(source, target, sems.at[index])
        for index, (source, target) in enumerate(
            [
                (cv_hbm, value_ref.at[:cache_rows]),
                (nv_hbm, value_ref.at[cache_rows:]),
                (ck_hbm, out_ref.at[:cache_rows]),
                (nk_hbm, out_ref.at[cache_rows:keys]),
            ]
        )
    ]
    for copy in copies:
        copy.start()
    for copy in copies[:2]:
        copy.wait()
    for g in range(KVH):
        out_ref[keys:, g * keys : (g + 1) * keys] = value_ref[:, g * HD : (g + 1) * HD].T
    for copy in copies[2:]:
        copy.wait()


def mask_columns(device, origin, window, cache_rows, prompt_rows, near):
    keys = cache_rows + prompt_rows
    key = lax.broadcasted_iota(jnp.int32, (keys, HD), 0)
    feature = lax.broadcasted_iota(jnp.int32, (keys, HD), 1)
    low = window[0] - origin * cache_rows
    high = jnp.minimum(window[1] - origin * cache_rows, cache_rows)
    top = jnp.where(origin > device, cache_rows, keys)
    cached = (key >= low) & (key < high)
    new = key >= cache_rows
    hidden = jnp.where(cached | new, 0.0, MASKED)
    shown = cached | (new & (key < top))
    masks = jnp.where(shown | (feature != prompt_rows), 0.0, MASKED)
    if near:
        late = (origin == device) & (feature < prompt_rows) & (key - cache_rows > feature)
        masks = jnp.where(late, MASKED, masks)
    return masks.astype(BF16), hidden


def row_features(rows, prompt_rows):
    feature = lax.broadcasted_iota(jnp.int32, (HD, rows), 0)
    row = lax.rem(lax.broadcasted_iota(jnp.int32, (HD, rows), 1), prompt_rows)
    return jnp.where((feature == row) | (feature == prompt_rows), 1.0, 0.0).astype(BF16)


def own_head(full, cont_rows):
    group = lax.broadcasted_iota(jnp.int32, (HD, KVH * cont_rows), 1) // cont_rows
    parts = [jnp.where(group == g, full[g * HD : (g + 1) * HD], 0.0) for g in range(KVH)]
    return jnp.concatenate([functools.reduce(jnp.add, parts), full[KVH * HD :]], axis=0)


def prep_kernel(
    length_hbm, query_hbm, cont_hbm, key_hbm, value_hbm,
    q_ref, cont_q_ref, cont_max_ref, cont_total_ref,
    length_ref, query_ref, cont_ref, key_ref, value_ref, sems,
):
    loads = [
        pltpu.make_async_copy(source, target, sems.at[index])
        for index, (source, target) in enumerate(
            [
                (query_hbm, query_ref), (cont_hbm, cont_ref), (key_hbm, key_ref),
                (value_hbm, value_ref), (length_hbm, length_ref),
            ]
        )
    ]
    for load in loads:
        load.start()
    prompt_rows = query_ref.shape[0]
    cont_count, suffix_rows = key_ref.shape[:2]
    cont_rows = cont_count * GROUP
    dot = functools.partial(jnp.dot, preferred_element_type=F32)
    q_ref[KVH * HD :] = row_features(GROUP * prompt_rows, prompt_rows)
    heads = [slice(head * HD, (head + 1) * HD) for head in range(KVH * GROUP)]
    for load in loads[:2]:
        load.wait()
    for g in range(KVH):
        q = jnp.concatenate([query_ref[:, head] for head in heads[g * GROUP : (g + 1) * GROUP]], axis=0)
        q_ref[g * HD : (g + 1) * HD] = q.T
    cont = cont_ref[...].astype(F32)
    cont_q = jnp.concatenate(
        [
            cont[c : c + 1, head]
            for g in range(KVH)
            for c in range(cont_count)
            for head in heads[g * GROUP : (g + 1) * GROUP]
        ],
        axis=0,
    ).T
    column = lax.broadcasted_iota(jnp.int32, cont_q.shape, 1) // cont_rows
    cont_q = jnp.concatenate([jnp.where(column == g, cont_q, 0.0) for g in range(KVH)], axis=0)
    cont_q = cont_q.astype(BF16)
    cont_q_ref[...] = cont_q
    for load in loads[2:]:
        load.wait()
    scores = [dot(key_ref[c], cont_q) for c in range(cont_count)]
    v = value_ref[...].reshape(cont_count * suffix_rows, KVH * HD).T
    v = jnp.concatenate([v, jnp.ones((ONES, v.shape[1]), BF16)], axis=0)
    key = lax.broadcasted_iota(jnp.int32, scores[0].shape, 0)
    owner = lax.broadcasted_iota(jnp.int32, scores[0].shape, 1) % cont_rows // GROUP
    s = jnp.concatenate(
        [
            jnp.where((owner == c) & (key < length_ref[c]), scores[c], MASKED)
            for c in range(cont_count)
        ],
        axis=0,
    )
    new_max, p, _ = weigh(s, FLOOR)
    cont_max_ref[...] = new_max
    cont_total_ref[...] = own_head(dot(v, p), cont_rows)


def window_kernel(first_ref, last_ref, window_ref):
    window_ref[0:1] = jnp.full((1, HD), first_ref[0], jnp.int32)
    window_ref[1:2] = jnp.full((1, HD), last_ref[0], jnp.int32)


def weigh(scores, old_max):
    new_max = jnp.maximum(old_max, jnp.max(scores, axis=0, keepdims=True))
    p = jnp.exp2((scores - new_max) * SCALE).astype(BF16)
    return new_max, p, jnp.exp2((old_max - new_max) * SCALE)


def take_kernel(size, cache_rows, prompt_rows, cont_count, sources, kind, *refs):
    first, last = kind == "first", kind == "last"
    window_ref, q_ref, cont_q_ref = refs[:3]
    held, refs = (refs[3:5], refs[5:]) if first else (refs[3:7], refs[7:])
    blocks, outs = refs[: len(sources)], refs[len(sources) :]
    device = lax.axis_index("ctx")
    keys = cache_rows + prompt_rows
    cont_rows = cont_count * GROUP
    ones = jnp.ones((ONES, len(blocks) * keys), BF16)
    dot = functools.partial(jnp.dot, preferred_element_type=F32)
    if last:
        out_hbm, cont_hbm, out_ref, cont_ref, sems = outs

    window = (window_ref[0:1], window_ref[1:2])
    terms = [
        mask_columns(
            device, block_origin(device, *source, size), window, cache_rows, prompt_rows, source[0] == 0
        )
        for source in sources
    ]
    masks = jnp.concatenate([term[0] for term in terms], axis=0)
    hidden = jnp.concatenate([term[1][:, :1] for term in terms], axis=0)
    values = [
        jnp.concatenate([block[keys:, g * keys : (g + 1) * keys] for block in blocks], axis=1)
        for g in range(KVH)
    ]
    stores = []

    def cont_scores():
        cuts = [slice(at, at + 2 * HD) for at in range(0, KVH * HD, 2 * HD)]
        parts = [
            dot(jnp.concatenate([block[:keys, cut] for block in blocks], axis=0), cont_q_ref[cut])
            for cut in cuts
        ]
        return sum(parts) + hidden

    def finish_cont(s):
        new_max, p, old = weigh(s, held[0][...])
        total = own_head(dot(jnp.concatenate(values + [ones], axis=0), p), cont_rows)
        total = total + held[1][...] * old
        if not last:
            outs[0][...] = new_max
            outs[1][...] = total
            return
        result = (total[:HD] * (1.0 / total[HD : HD + 1])).T
        for row in range(KVH * cont_rows):
            g, c, h = row // cont_rows, row % cont_rows // GROUP, row % GROUP
            cols = slice((g * GROUP + h) * HD, (g * GROUP + h + 1) * HD)
            cont_ref[c : c + 1, cols] = result[row : row + 1].astype(BF16)
        stores.append(pltpu.make_async_copy(cont_ref, cont_hbm, sems.at[KVH]))
        stores[-1].start()

    def head_scores(g):
        cols = slice(g * HD, (g + 1) * HD)
        k = jnp.concatenate([block[:keys, cols] for block in blocks], axis=0)
        q = jnp.concatenate([q_ref[cols], q_ref[KVH * HD :]], axis=0)
        return dot(jnp.concatenate([k, masks], axis=1), q)

    def finish_head(g, s):
        new_max, p, old = weigh(s, FLOOR if first else held[2][g])
        total = dot(jnp.concatenate([values[g], ones], axis=0), p)
        if not first:
            total = total + held[3][g] * old
        if not last:
            outs[2][g] = new_max
            outs[3][g] = total
            return
        result = (total[:HD] * (1.0 / total[HD : HD + 1])).T.astype(BF16)
        for h in range(GROUP):
            cols = slice((g * GROUP + h) * HD, (g * GROUP + h + 1) * HD)
            out_ref[:, cols] = result[h * prompt_rows : (h + 1) * prompt_rows]
        cols = slice(g * GROUP * HD, (g + 1) * GROUP * HD)
        stores.append(
            pltpu.make_async_copy(out_ref.at[:, cols], out_hbm.at[:, cols], sems.at[g])
        )
        stores[-1].start()

    work = [(cont_scores, finish_cont)] + [
        (functools.partial(head_scores, g), functools.partial(finish_head, g)) for g in range(KVH)
    ]
    ready = [scores() for scores, _ in work[:AHEAD]]
    for index, (_, finish) in enumerate(work):
        if index + AHEAD < len(work):
            ready.append(work[index + AHEAD][0]())
        finish(ready[index])
    for store in stores:
        store.wait()


def in_hbm(array):
    return pltpu.with_memory_space_constraint(array, pltpu.HBM)


def cost(rows, keys):
    work = rows * keys
    return pl.CostEstimate(flops=8 * work * HD, transcendentals=work, bytes_accessed=1 << 20)


def body(
    size,
    cache_keys,
    cache_values,
    new_queries,
    new_keys,
    new_values,
    cont_queries,
    suffix_keys,
    suffix_values,
    window_start,
    prefix_length,
    suffix_length,
):
    cache_rows, prompt_rows, cont_count = (
        cache_keys.shape[0], new_keys.shape[0], cont_queries.shape[0],
    )
    keys = cache_rows + prompt_rows
    chips = size // 2
    ring = ring_pairs(size)
    pair = [(device, device ^ 1) for device in range(size)]
    params = pltpu.CompilerParams(vmem_limit_bytes=24 << 20)
    rows, cont_rows = GROUP * prompt_rows, KVH * GROUP * cont_count
    shape = jax.ShapeDtypeStruct

    def send(block, pairs):
        return lax.ppermute(block, "ctx", pairs)

    own = pl.pallas_call(
        pack_kernel,
        out_shape=shape((keys + HD, KVH * HD), BF16),
        in_specs=[HBM] * 4,
        out_specs=VMEM,
        scratch_shapes=[pltpu.VMEM((keys, KVH * HD), BF16), pltpu.SemaphoreType.DMA((4,))],
        compiler_params=params,
    )(*[in_hbm(x) for x in (cache_keys, new_keys, cache_values, new_values)])
    other = send(own, pair)
    waiting = [((0, False, False), own), ((0, False, True), other)]

    state_shape = [
        shape((1, cont_rows), F32),
        shape((HD + ONES, cont_rows), F32),
        shape((KVH, 1, rows), F32),
        shape((KVH, HD + ONES, rows), F32),
    ]
    queries, cont_q, *state = pl.pallas_call(
        prep_kernel,
        out_shape=[
            shape(((KVH + 1) * HD, rows), BF16),
            shape((KVH * HD, cont_rows), BF16),
        ] + state_shape[:2],
        in_specs=[HBM] * 5,
        out_specs=[VMEM] * 4,
        scratch_shapes=[
            pltpu.SMEM(suffix_length.shape, jnp.int32),
            pltpu.VMEM(new_queries.shape, BF16),
            pltpu.VMEM(cont_queries.shape, BF16),
            pltpu.VMEM(suffix_keys.shape, BF16),
            pltpu.VMEM(suffix_values.shape, BF16),
            pltpu.SemaphoreType.DMA((5,)),
        ],
        compiler_params=params,
        cost_estimate=cost(rows, keys),
    )(*[in_hbm(x) for x in (suffix_length, new_queries, cont_queries, suffix_keys, suffix_values)])

    window = pl.pallas_call(
        window_kernel,
        out_shape=shape((2, HD), jnp.int32),
        in_specs=[SMEM] * 2,
        out_specs=VMEM,
        compiler_params=params,
    )(window_start, prefix_length)

    def take(state, held, kind="middle"):
        sources, blocks = zip(*held)
        specs, scratch, outs = [VMEM] * 4, [], state_shape
        if kind == "last":
            outs = [shape(new_queries.shape, BF16), shape(cont_queries.shape, BF16)]
            specs = [HBM] * 2
            scratch = [
                pltpu.VMEM(new_queries.shape, BF16),
                pltpu.VMEM(cont_queries.shape, BF16),
                pltpu.SemaphoreType.DMA((KVH + 1,)),
            ]
        aliases = {} if kind == "last" else {3 + index: index for index in range(len(state))}
        return pl.pallas_call(
            functools.partial(
                take_kernel, size, cache_rows, prompt_rows, cont_count, sources, kind
            ),
            out_shape=outs,
            in_specs=[VMEM] * (3 + len(state) + len(blocks)),
            out_specs=specs,
            scratch_shapes=scratch,
            input_output_aliases=aliases,
            compiler_params=params,
            cost_estimate=cost(rows, len(blocks) * keys),
        )(window, queries, cont_q, *state, *blocks)

    hops = chips // 2
    for hop in range(1, hops):
        own, other = send(own, ring), send(other, ring)
        swap, swop = send(own, pair), send(other, pair)
        arrived = [((hop, False, False), own), ((hop, True, False), swap)]
        if hop == 1:
            state = take(state, waiting, "first")
            waiting = []
        else:
            state = take(state, waiting[:2])
            waiting = waiting[2:]
            if hop + 1 == hops:
                waiting, arrived = waiting + arrived, []
            state = take(state, waiting)
            waiting = []
        waiting += arrived + [((hop, False, True), other), ((hop, True, True), swop)]
    own = send(own, ring)
    swapped = send(own, pair)
    state = take(state, waiting + [((hops, False, False), own)])
    return tuple(take(state, [((hops, True, False), swapped)], "last"))


def solution(mesh):
    in_specs = (
        P(("grp", "ctx"), None),
        P(("grp", "ctx"), None),
        P(("grp", "ctx"), None),
        P(("grp", "ctx"), None),
        P(("grp", "ctx"), None),
        P(("grp", "ctx"), None),
        P(("grp", "ctx"), None, None),
        P(("grp", "ctx"), None, None),
        P("grp"),
        P("grp"),
        P(("grp", "ctx")),
    )
    out_specs = (P(("grp", "ctx"), None), P(("grp", "ctx"), None))
    size = mesh.shape["ctx"]

    def run(*arrays):
        return body(size, *arrays)

    return jax.shard_map(run, mesh=mesh, in_specs=in_specs, out_specs=out_specs, check_vma=False)
```

```python
import functools
import math

import jax
import jax.numpy as jnp
from jax import lax
from jax.experimental import pallas as pl
from jax.experimental.pallas import tpu as pltpu
from jax.sharding import PartitionSpec as P

KVH = 4
HD = 128
GROUP = 8
SCALE = HD ** (-0.5) * math.log2(math.e)
MASKED = -1e30
FLOOR = -1e20
ONES = 16
AHEAD = 3

VMEM = pl.BlockSpec(memory_space=pltpu.VMEM)
SMEM = pl.BlockSpec(memory_space=pltpu.SMEM)
HBM = pl.BlockSpec(memory_space=pltpu.HBM)
BF16 = jnp.bfloat16
F32 = jnp.float32


def ring_chip(place, chips):
    return jnp.where(place < chips // 2, 2 * place, 2 * (chips - 1 - place) + 1)


def ring_place(chip, chips):
    return jnp.where(chip % 2 == 0, chip // 2, chips - 1 - chip // 2)


def ring_pairs(size):
    chips = size // 2
    order = list(range(0, chips, 2)) + list(range(chips - 1, 0, -2))
    pairs = []
    for place, chip in enumerate(order):
        for way, step in enumerate((1, -1)):
            core = (place + way) % 2
            pairs.append((2 * chip + core, 2 * order[(place + step) % chips] + 1 - core))
    return sorted(pairs)


def block_origin(device, hop, swapped, partner, size):
    chips = size // 2
    chip, core = device // 2, device % 2
    place = ring_place(chip, chips)
    way = (core + place) % 2
    if swapped:
        way = 1 - way
    place = lax.rem(place + jnp.where(way == 0, -hop, hop) + 2 * chips, chips)
    held = (way + place) % 2
    if partner:
        held = 1 - held
    return 2 * ring_chip(place, chips) + held


def pack_kernel(ck_hbm, nk_hbm, cv_hbm, nv_hbm, out_ref, value_ref, sems):
    cache_rows, keys = ck_hbm.shape[0], value_ref.shape[0]
    copies = [
        pltpu.make_async_copy(source, target, sems.at[index])
        for index, (source, target) in enumerate(
            [
                (cv_hbm, value_ref.at[:cache_rows]),
                (nv_hbm, value_ref.at[cache_rows:]),
                (ck_hbm, out_ref.at[:cache_rows]),
                (nk_hbm, out_ref.at[cache_rows:keys]),
            ]
        )
    ]
    for copy in copies:
        copy.start()
    for copy in copies[:2]:
        copy.wait()
    for g in range(KVH):
        out_ref[keys:, g * keys : (g + 1) * keys] = value_ref[:, g * HD : (g + 1) * HD].T
    for copy in copies[2:]:
        copy.wait()


def mask_columns(device, origin, window, cache_rows, prompt_rows, near):
    keys = cache_rows + prompt_rows
    key = lax.broadcasted_iota(jnp.int32, (keys, HD), 0)
    feature = lax.broadcasted_iota(jnp.int32, (keys, HD), 1)
    low = window[0] - origin * cache_rows
    high = jnp.minimum(window[1] - origin * cache_rows, cache_rows)
    top = jnp.where(origin > device, cache_rows, keys)
    cached = (key >= low) & (key < high)
    new = key >= cache_rows
    hidden = jnp.where(cached | new, 0.0, MASKED)
    shown = cached | (new & (key < top))
    masks = jnp.where(shown | (feature != prompt_rows), 0.0, MASKED)
    if near:
        late = (origin == device) & (feature < prompt_rows) & (key - cache_rows > feature)
        masks = jnp.where(late, MASKED, masks)
    return masks.astype(BF16), hidden


def row_features(rows, prompt_rows):
    feature = lax.broadcasted_iota(jnp.int32, (HD, rows), 0)
    row = lax.rem(lax.broadcasted_iota(jnp.int32, (HD, rows), 1), prompt_rows)
    return jnp.where((feature == row) | (feature == prompt_rows), 1.0, 0.0).astype(BF16)


def own_head(full, cont_rows):
    group = lax.broadcasted_iota(jnp.int32, (HD, KVH * cont_rows), 1) // cont_rows
    parts = [jnp.where(group == g, full[g * HD : (g + 1) * HD], 0.0) for g in range(KVH)]
    return jnp.concatenate([functools.reduce(jnp.add, parts), full[KVH * HD :]], axis=0)


def prep_kernel(
    length_hbm, query_hbm, cont_hbm, key_hbm, value_hbm,
    q_ref, cont_q_ref, cont_max_ref, cont_total_ref,
    length_ref, query_ref, cont_ref, key_ref, value_ref, sems,
):
    loads = [
        pltpu.make_async_copy(source, target, sems.at[index])
        for index, (source, target) in enumerate(
            [
                (query_hbm, query_ref), (cont_hbm, cont_ref), (key_hbm, key_ref),
                (value_hbm, value_ref), (length_hbm, length_ref),
            ]
        )
    ]
    for load in loads:
        load.start()
    prompt_rows = query_ref.shape[0]
    cont_count, suffix_rows = key_ref.shape[:2]
    cont_rows = cont_count * GROUP
    dot = functools.partial(jnp.dot, preferred_element_type=F32)
    q_ref[KVH * HD :] = row_features(GROUP * prompt_rows, prompt_rows)
    heads = [slice(head * HD, (head + 1) * HD) for head in range(KVH * GROUP)]
    for load in loads[:2]:
        load.wait()
    for g in range(KVH):
        q = jnp.concatenate([query_ref[:, head] for head in heads[g * GROUP : (g + 1) * GROUP]], axis=0)
        q_ref[g * HD : (g + 1) * HD] = q.T
    cont = cont_ref[...].astype(F32)
    cont_q = jnp.concatenate(
        [
            cont[c : c + 1, head]
            for g in range(KVH)
            for c in range(cont_count)
            for head in heads[g * GROUP : (g + 1) * GROUP]
        ],
        axis=0,
    ).T
    column = lax.broadcasted_iota(jnp.int32, cont_q.shape, 1) // cont_rows
    cont_q = jnp.concatenate([jnp.where(column == g, cont_q, 0.0) for g in range(KVH)], axis=0)
    cont_q = cont_q.astype(BF16)
    cont_q_ref[...] = cont_q
    for load in loads[2:]:
        load.wait()
    scores = [dot(key_ref[c], cont_q) for c in range(cont_count)]
    v = value_ref[...].reshape(cont_count * suffix_rows, KVH * HD).T
    v = jnp.concatenate([v, jnp.ones((ONES, v.shape[1]), BF16)], axis=0)
    key = lax.broadcasted_iota(jnp.int32, scores[0].shape, 0)
    owner = lax.broadcasted_iota(jnp.int32, scores[0].shape, 1) % cont_rows // GROUP
    s = jnp.concatenate(
        [
            jnp.where((owner == c) & (key < length_ref[c]), scores[c], MASKED)
            for c in range(cont_count)
        ],
        axis=0,
    )
    new_max, p, _ = weigh(s, FLOOR)
    cont_max_ref[...] = new_max
    cont_total_ref[...] = own_head(dot(v, p), cont_rows)


def window_kernel(first_ref, last_ref, window_ref):
    window_ref[0:1] = jnp.full((1, HD), first_ref[0], jnp.int32)
    window_ref[1:2] = jnp.full((1, HD), last_ref[0], jnp.int32)


def weigh(scores, old_max):
    new_max = jnp.maximum(old_max, jnp.max(scores, axis=0, keepdims=True))
    p = jnp.exp2((scores - new_max) * SCALE).astype(BF16)
    return new_max, p, jnp.exp2((old_max - new_max) * SCALE)


def take_kernel(size, cache_rows, prompt_rows, cont_count, sources, kind, *refs):
    first, last = kind == "first", kind == "last"
    window_ref, q_ref, cont_q_ref = refs[:3]
    held, refs = (refs[3:5], refs[5:]) if first else (refs[3:7], refs[7:])
    blocks, outs = refs[: len(sources)], refs[len(sources) :]
    device = lax.axis_index("ctx")
    keys = cache_rows + prompt_rows
    cont_rows = cont_count * GROUP
    ones = jnp.ones((ONES, len(blocks) * keys), BF16)
    dot = functools.partial(jnp.dot, preferred_element_type=F32)
    if last:
        out_hbm, cont_hbm, out_ref, cont_ref, sems = outs

    window = (window_ref[0:1], window_ref[1:2])
    terms = [
        mask_columns(
            device, block_origin(device, *source, size), window, cache_rows, prompt_rows, source[0] == 0
        )
        for source in sources
    ]
    masks = jnp.concatenate([term[0] for term in terms], axis=0)
    hidden = jnp.concatenate([term[1][:, :1] for term in terms], axis=0)
    values = [
        jnp.concatenate([block[keys:, g * keys : (g + 1) * keys] for block in blocks], axis=1)
        for g in range(KVH)
    ]
    stores = []

    def cont_scores():
        cuts = [slice(at, at + 2 * HD) for at in range(0, KVH * HD, 2 * HD)]
        parts = [
            dot(jnp.concatenate([block[:keys, cut] for block in blocks], axis=0), cont_q_ref[cut])
            for cut in cuts
        ]
        return sum(parts) + hidden

    def finish_cont(s):
        new_max, p, old = weigh(s, held[0][...])
        total = own_head(dot(jnp.concatenate(values + [ones], axis=0), p), cont_rows)
        total = total + held[1][...] * old
        if not last:
            outs[0][...] = new_max
            outs[1][...] = total
            return
        result = (total[:HD] * (1.0 / total[HD : HD + 1])).T
        for row in range(KVH * cont_rows):
            g, c, h = row // cont_rows, row % cont_rows // GROUP, row % GROUP
            cols = slice((g * GROUP + h) * HD, (g * GROUP + h + 1) * HD)
            cont_ref[c : c + 1, cols] = result[row : row + 1].astype(BF16)
        stores.append(pltpu.make_async_copy(cont_ref, cont_hbm, sems.at[KVH]))
        stores[-1].start()

    def head_scores(g):
        cols = slice(g * HD, (g + 1) * HD)
        k = jnp.concatenate([block[:keys, cols] for block in blocks], axis=0)
        q = jnp.concatenate([q_ref[cols], q_ref[KVH * HD :]], axis=0)
        return dot(jnp.concatenate([k, masks], axis=1), q)

    def finish_head(g, s):
        new_max, p, old = weigh(s, FLOOR if first else held[2][g])
        total = dot(jnp.concatenate([values[g], ones], axis=0), p)
        if not first:
            total = total + held[3][g] * old
        if not last:
            outs[2][g] = new_max
            outs[3][g] = total
            return
        result = (total[:HD] * (1.0 / total[HD : HD + 1])).T.astype(BF16)
        for h in range(GROUP):
            cols = slice((g * GROUP + h) * HD, (g * GROUP + h + 1) * HD)
            out_ref[:, cols] = result[h * prompt_rows : (h + 1) * prompt_rows]
        cols = slice(g * GROUP * HD, (g + 1) * GROUP * HD)
        stores.append(
            pltpu.make_async_copy(out_ref.at[:, cols], out_hbm.at[:, cols], sems.at[g])
        )
        stores[-1].start()

    work = [(cont_scores, finish_cont)] + [
        (functools.partial(head_scores, g), functools.partial(finish_head, g)) for g in range(KVH)
    ]
    ready = [scores() for scores, _ in work[:AHEAD]]
    for index, (_, finish) in enumerate(work):
        if index + AHEAD < len(work):
            ready.append(work[index + AHEAD][0]())
        finish(ready[index])
    for store in stores:
        store.wait()


def in_hbm(array):
    return pltpu.with_memory_space_constraint(array, pltpu.HBM)


def cost(rows, keys):
    work = rows * keys
    return pl.CostEstimate(flops=8 * work * HD, transcendentals=work, bytes_accessed=1 << 20)


def body(
    size,
    cache_keys,
    cache_values,
    new_queries,
    new_keys,
    new_values,
    cont_queries,
    suffix_keys,
    suffix_values,
    window_start,
    prefix_length,
    suffix_length,
):
    cache_rows, prompt_rows, cont_count = (
        cache_keys.shape[0], new_keys.shape[0], cont_queries.shape[0],
    )
    keys = cache_rows + prompt_rows
    chips = size // 2
    ring = ring_pairs(size)
    pair = [(device, device ^ 1) for device in range(size)]
    params = pltpu.CompilerParams(vmem_limit_bytes=24 << 20)
    rows, cont_rows = GROUP * prompt_rows, KVH * GROUP * cont_count
    shape = jax.ShapeDtypeStruct

    def send(block, pairs):
        return lax.ppermute(block, "ctx", pairs)

    own = pl.pallas_call(
        pack_kernel,
        out_shape=shape((keys + HD, KVH * HD), BF16),
        in_specs=[HBM] * 4,
        out_specs=VMEM,
        scratch_shapes=[pltpu.VMEM((keys, KVH * HD), BF16), pltpu.SemaphoreType.DMA((4,))],
        compiler_params=params,
    )(*[in_hbm(x) for x in (cache_keys, new_keys, cache_values, new_values)])
    other = send(own, pair)
    waiting = [((0, False, False), own), ((0, False, True), other)]

    state_shape = [
        shape((1, cont_rows), F32),
        shape((HD + ONES, cont_rows), F32),
        shape((KVH, 1, rows), F32),
        shape((KVH, HD + ONES, rows), F32),
    ]
    queries, cont_q, *state = pl.pallas_call(
        prep_kernel,
        out_shape=[
            shape(((KVH + 1) * HD, rows), BF16),
            shape((KVH * HD, cont_rows), BF16),
        ] + state_shape[:2],
        in_specs=[HBM] * 5,
        out_specs=[VMEM] * 4,
        scratch_shapes=[
            pltpu.SMEM(suffix_length.shape, jnp.int32),
            pltpu.VMEM(new_queries.shape, BF16),
            pltpu.VMEM(cont_queries.shape, BF16),
            pltpu.VMEM(suffix_keys.shape, BF16),
            pltpu.VMEM(suffix_values.shape, BF16),
            pltpu.SemaphoreType.DMA((5,)),
        ],
        compiler_params=params,
        cost_estimate=cost(rows, keys),
    )(*[in_hbm(x) for x in (suffix_length, new_queries, cont_queries, suffix_keys, suffix_values)])

    window = pl.pallas_call(
        window_kernel,
        out_shape=shape((2, HD), jnp.int32),
        in_specs=[SMEM] * 2,
        out_specs=VMEM,
        compiler_params=params,
    )(window_start, prefix_length)

    def take(state, held, kind="middle"):
        sources, blocks = zip(*held)
        specs, scratch, outs = [VMEM] * 4, [], state_shape
        if kind == "last":
            outs = [shape(new_queries.shape, BF16), shape(cont_queries.shape, BF16)]
            specs = [HBM] * 2
            scratch = [
                pltpu.VMEM(new_queries.shape, BF16),
                pltpu.VMEM(cont_queries.shape, BF16),
                pltpu.SemaphoreType.DMA((KVH + 1,)),
            ]
        aliases = {} if kind == "last" else {3 + index: index for index in range(len(state))}
        return pl.pallas_call(
            functools.partial(
                take_kernel, size, cache_rows, prompt_rows, cont_count, sources, kind
            ),
            out_shape=outs,
            in_specs=[VMEM] * (3 + len(state) + len(blocks)),
            out_specs=specs,
            scratch_shapes=scratch,
            input_output_aliases=aliases,
            compiler_params=params,
            cost_estimate=cost(rows, len(blocks) * keys),
        )(window, queries, cont_q, *state, *blocks)

    hops = chips // 2
    for hop in range(1, hops):
        own, other = send(own, ring), send(other, ring)
        swap, swop = send(own, pair), send(other, pair)
        state = take(state, waiting, "first" if hop == 1 else "middle")
        arrived = [((hop, False, False), own), ((hop, True, False), swap)]
        waiting = [((hop, False, True), other), ((hop, True, True), swop)]
        if hop + 1 == hops:
            arrived, waiting = arrived + waiting[:1], waiting[1:]
        state = take(state, arrived)
    own = send(own, ring)
    swapped = send(own, pair)
    state = take(state, waiting + [((hops, False, False), own)])
    return tuple(take(state, [((hops, True, False), swapped)], "last"))


def solution(mesh):
    in_specs = (
        P(("grp", "ctx"), None),
        P(("grp", "ctx"), None),
        P(("grp", "ctx"), None),
        P(("grp", "ctx"), None),
        P(("grp", "ctx"), None),
        P(("grp", "ctx"), None),
        P(("grp", "ctx"), None, None),
        P(("grp", "ctx"), None, None),
        P("grp"),
        P("grp"),
        P(("grp", "ctx")),
    )
    out_specs = (P(("grp", "ctx"), None), P(("grp", "ctx"), None))
    size = mesh.shape["ctx"]

    def run(*arrays):
        return body(size, *arrays)

    return jax.shard_map(run, mesh=mesh, in_specs=in_specs, out_specs=out_specs, check_vma=False)
```

```python
import functools
import math

import jax
import jax.numpy as jnp
from jax import lax
from jax.experimental import pallas as pl
from jax.experimental.pallas import tpu as pltpu
from jax.sharding import PartitionSpec as P

KVH = 4
HD = 128
GROUP = 8
SCALE = HD ** (-0.5) * math.log2(math.e)
MASKED = -1e30
FLOOR = -1e20
ONES = 16
AHEAD = 3

VMEM = pl.BlockSpec(memory_space=pltpu.VMEM)
SMEM = pl.BlockSpec(memory_space=pltpu.SMEM)
HBM = pl.BlockSpec(memory_space=pltpu.HBM)
BF16 = jnp.bfloat16
F32 = jnp.float32


def ring_chip(place, chips):
    return jnp.where(place < chips // 2, 2 * place, 2 * (chips - 1 - place) + 1)


def ring_place(chip, chips):
    return jnp.where(chip % 2 == 0, chip // 2, chips - 1 - chip // 2)


def ring_pairs(size):
    chips = size // 2
    order = list(range(0, chips, 2)) + list(range(chips - 1, 0, -2))
    pairs = []
    for place, chip in enumerate(order):
        for way, step in enumerate((1, -1)):
            core = (place + way) % 2
            pairs.append((2 * chip + core, 2 * order[(place + step) % chips] + 1 - core))
    return sorted(pairs)


def block_origin(device, hop, swapped, partner, size):
    chips = size // 2
    chip, core = device // 2, device % 2
    place = ring_place(chip, chips)
    way = (core + place) % 2
    if swapped:
        way = 1 - way
    place = lax.rem(place + jnp.where(way == 0, -hop, hop) + 2 * chips, chips)
    held = (way + place) % 2
    if partner:
        held = 1 - held
    return 2 * ring_chip(place, chips) + held


def pack_kernel(ck_hbm, nk_hbm, cv_hbm, nv_hbm, out_ref, value_ref, sems):
    cache_rows, keys = ck_hbm.shape[0], value_ref.shape[0]
    copies = [
        pltpu.make_async_copy(source, target, sems.at[index])
        for index, (source, target) in enumerate(
            [
                (cv_hbm, value_ref.at[:cache_rows]),
                (nv_hbm, value_ref.at[cache_rows:]),
                (ck_hbm, out_ref.at[:cache_rows]),
                (nk_hbm, out_ref.at[cache_rows:keys]),
            ]
        )
    ]
    for copy in copies:
        copy.start()
    for copy in copies[:2]:
        copy.wait()
    for g in range(KVH):
        out_ref[keys:, g * keys : (g + 1) * keys] = value_ref[:, g * HD : (g + 1) * HD].T
    for copy in copies[2:]:
        copy.wait()


def mask_columns(device, origin, window, cache_rows, prompt_rows, near):
    keys = cache_rows + prompt_rows
    key = lax.broadcasted_iota(jnp.int32, (keys, HD), 0)
    feature = lax.broadcasted_iota(jnp.int32, (keys, HD), 1)
    low = window[0] - origin * cache_rows
    high = jnp.minimum(window[1] - origin * cache_rows, cache_rows)
    top = jnp.where(origin > device, cache_rows, keys)
    cached = (key >= low) & (key < high)
    new = key >= cache_rows
    hidden = jnp.where(cached | new, 0.0, MASKED)
    shown = cached | (new & (key < top))
    masks = jnp.where(shown | (feature != prompt_rows), 0.0, MASKED)
    if near:
        late = (origin == device) & (feature < prompt_rows) & (key - cache_rows > feature)
        masks = jnp.where(late, MASKED, masks)
    return masks.astype(BF16), hidden


def row_features(rows, prompt_rows):
    feature = lax.broadcasted_iota(jnp.int32, (HD, rows), 0)
    row = lax.rem(lax.broadcasted_iota(jnp.int32, (HD, rows), 1), prompt_rows)
    return jnp.where((feature == row) | (feature == prompt_rows), 1.0, 0.0).astype(BF16)


def own_head(full, cont_rows):
    group = lax.broadcasted_iota(jnp.int32, (HD, KVH * cont_rows), 1) // cont_rows
    parts = [jnp.where(group == g, full[g * HD : (g + 1) * HD], 0.0) for g in range(KVH)]
    return jnp.concatenate([functools.reduce(jnp.add, parts), full[KVH * HD :]], axis=0)


def prep_kernel(
    length_hbm, query_hbm, cont_hbm, key_hbm, value_hbm,
    q_ref, cont_q_ref, cont_max_ref, cont_total_ref,
    length_ref, query_ref, cont_ref, key_ref, value_ref, sems,
):
    loads = [
        pltpu.make_async_copy(source, target, sems.at[index])
        for index, (source, target) in enumerate(
            [
                *[
                    (query_hbm.at[:, cols], query_ref.at[:, cols])
                    for cols in (
                        slice(g * GROUP * HD, (g + 1) * GROUP * HD) for g in range(KVH)
                    )
                ],
                (cont_hbm, cont_ref), (key_hbm, key_ref), (value_hbm, value_ref),
                (length_hbm, length_ref),
            ]
        )
    ]
    for load in loads:
        load.start()
    prompt_rows = query_ref.shape[0]
    cont_count, suffix_rows = key_ref.shape[:2]
    cont_rows = cont_count * GROUP
    dot = functools.partial(jnp.dot, preferred_element_type=F32)
    q_ref[KVH * HD :] = row_features(GROUP * prompt_rows, prompt_rows)
    heads = [slice(head * HD, (head + 1) * HD) for head in range(KVH * GROUP)]
    for g in range(KVH):
        loads[g].wait()
        q = jnp.concatenate([query_ref[:, head] for head in heads[g * GROUP : (g + 1) * GROUP]], axis=0)
        q_ref[g * HD : (g + 1) * HD] = q.T
    loads[KVH].wait()
    cont = cont_ref[...].astype(F32)
    cont_q = jnp.concatenate(
        [
            cont[c : c + 1, head]
            for g in range(KVH)
            for c in range(cont_count)
            for head in heads[g * GROUP : (g + 1) * GROUP]
        ],
        axis=0,
    ).T
    column = lax.broadcasted_iota(jnp.int32, cont_q.shape, 1) // cont_rows
    cont_q = jnp.concatenate([jnp.where(column == g, cont_q, 0.0) for g in range(KVH)], axis=0)
    cont_q = cont_q.astype(BF16)
    cont_q_ref[...] = cont_q
    for load in loads[KVH + 1 :]:
        load.wait()
    scores = [dot(key_ref[c], cont_q) for c in range(cont_count)]
    v = value_ref[...].reshape(cont_count * suffix_rows, KVH * HD).T
    v = jnp.concatenate([v, jnp.ones((ONES, v.shape[1]), BF16)], axis=0)
    key = lax.broadcasted_iota(jnp.int32, scores[0].shape, 0)
    owner = lax.broadcasted_iota(jnp.int32, scores[0].shape, 1) % cont_rows // GROUP
    s = jnp.concatenate(
        [
            jnp.where((owner == c) & (key < length_ref[c]), scores[c], MASKED)
            for c in range(cont_count)
        ],
        axis=0,
    )
    new_max, p, _ = weigh(s, FLOOR)
    cont_max_ref[...] = new_max
    cont_total_ref[...] = own_head(dot(v, p), cont_rows)


def window_kernel(first_ref, last_ref, window_ref):
    window_ref[0:1] = jnp.full((1, HD), first_ref[0], jnp.int32)
    window_ref[1:2] = jnp.full((1, HD), last_ref[0], jnp.int32)


def weigh(scores, old_max):
    new_max = jnp.maximum(old_max, jnp.max(scores, axis=0, keepdims=True))
    p = jnp.exp2((scores - new_max) * SCALE).astype(BF16)
    return new_max, p, jnp.exp2((old_max - new_max) * SCALE)


def take_kernel(size, cache_rows, prompt_rows, cont_count, sources, kind, *refs):
    first, last = kind == "first", kind == "last"
    window_ref, q_ref, cont_q_ref = refs[:3]
    held, refs = (refs[3:5], refs[5:]) if first else (refs[3:7], refs[7:])
    blocks, outs = refs[: len(sources)], refs[len(sources) :]
    device = lax.axis_index("ctx")
    keys = cache_rows + prompt_rows
    cont_rows = cont_count * GROUP
    ones = jnp.ones((ONES, len(blocks) * keys), BF16)
    dot = functools.partial(jnp.dot, preferred_element_type=F32)
    if last:
        out_hbm, cont_hbm, out_ref, cont_ref, sems = outs

    window = (window_ref[0:1], window_ref[1:2])
    terms = [
        mask_columns(
            device, block_origin(device, *source, size), window, cache_rows, prompt_rows, source[0] == 0
        )
        for source in sources
    ]
    masks = jnp.concatenate([term[0] for term in terms], axis=0)
    hidden = jnp.concatenate([term[1][:, :1] for term in terms], axis=0)
    values = [
        jnp.concatenate([block[keys:, g * keys : (g + 1) * keys] for block in blocks], axis=1)
        for g in range(KVH)
    ]
    stores = []

    def cont_scores():
        cuts = [slice(at, at + 2 * HD) for at in range(0, KVH * HD, 2 * HD)]
        parts = [
            dot(jnp.concatenate([block[:keys, cut] for block in blocks], axis=0), cont_q_ref[cut])
            for cut in cuts
        ]
        return sum(parts) + hidden

    def finish_cont(s):
        new_max, p, old = weigh(s, held[0][...])
        total = own_head(dot(jnp.concatenate(values + [ones], axis=0), p), cont_rows)
        total = total + held[1][...] * old
        if not last:
            outs[0][...] = new_max
            outs[1][...] = total
            return
        result = (total[:HD] * (1.0 / total[HD : HD + 1])).T
        for row in range(KVH * cont_rows):
            g, c, h = row // cont_rows, row % cont_rows // GROUP, row % GROUP
            cols = slice((g * GROUP + h) * HD, (g * GROUP + h + 1) * HD)
            cont_ref[c : c + 1, cols] = result[row : row + 1].astype(BF16)
        stores.append(pltpu.make_async_copy(cont_ref, cont_hbm, sems.at[KVH]))
        stores[-1].start()

    def head_scores(g):
        cols = slice(g * HD, (g + 1) * HD)
        k = jnp.concatenate([block[:keys, cols] for block in blocks], axis=0)
        q = jnp.concatenate([q_ref[cols], q_ref[KVH * HD :]], axis=0)
        return dot(jnp.concatenate([k, masks], axis=1), q)

    def finish_head(g, s):
        new_max, p, old = weigh(s, FLOOR if first else held[2][g])
        total = dot(jnp.concatenate([values[g], ones], axis=0), p)
        if not first:
            total = total + held[3][g] * old
        if not last:
            outs[2][g] = new_max
            outs[3][g] = total
            return
        result = (total[:HD] * (1.0 / total[HD : HD + 1])).T.astype(BF16)
        for h in range(GROUP):
            cols = slice((g * GROUP + h) * HD, (g * GROUP + h + 1) * HD)
            out_ref[:, cols] = result[h * prompt_rows : (h + 1) * prompt_rows]
        cols = slice(g * GROUP * HD, (g + 1) * GROUP * HD)
        stores.append(
            pltpu.make_async_copy(out_ref.at[:, cols], out_hbm.at[:, cols], sems.at[g])
        )
        stores[-1].start()

    work = [(cont_scores, finish_cont)] + [
        (functools.partial(head_scores, g), functools.partial(finish_head, g)) for g in range(KVH)
    ]
    ready = [scores() for scores, _ in work[:AHEAD]]
    for index, (_, finish) in enumerate(work):
        if index + AHEAD < len(work):
            ready.append(work[index + AHEAD][0]())
        finish(ready[index])
    for store in stores:
        store.wait()


def in_hbm(array):
    return pltpu.with_memory_space_constraint(array, pltpu.HBM)


def cost(rows, keys):
    work = rows * keys
    return pl.CostEstimate(flops=8 * work * HD, transcendentals=work, bytes_accessed=1 << 20)


def body(
    size,
    cache_keys,
    cache_values,
    new_queries,
    new_keys,
    new_values,
    cont_queries,
    suffix_keys,
    suffix_values,
    window_start,
    prefix_length,
    suffix_length,
):
    cache_rows, prompt_rows, cont_count = (
        cache_keys.shape[0], new_keys.shape[0], cont_queries.shape[0],
    )
    keys = cache_rows + prompt_rows
    chips = size // 2
    ring = ring_pairs(size)
    pair = [(device, device ^ 1) for device in range(size)]
    params = pltpu.CompilerParams(vmem_limit_bytes=24 << 20)
    rows, cont_rows = GROUP * prompt_rows, KVH * GROUP * cont_count
    shape = jax.ShapeDtypeStruct

    def send(block, pairs):
        return lax.ppermute(block, "ctx", pairs)

    own = pl.pallas_call(
        pack_kernel,
        out_shape=shape((keys + HD, KVH * HD), BF16),
        in_specs=[HBM] * 4,
        out_specs=VMEM,
        scratch_shapes=[pltpu.VMEM((keys, KVH * HD), BF16), pltpu.SemaphoreType.DMA((4,))],
        compiler_params=params,
    )(*[in_hbm(x) for x in (cache_keys, new_keys, cache_values, new_values)])
    other = send(own, pair)
    waiting = [((0, False, False), own), ((0, False, True), other)]

    state_shape = [
        shape((1, cont_rows), F32),
        shape((HD + ONES, cont_rows), F32),
        shape((KVH, 1, rows), F32),
        shape((KVH, HD + ONES, rows), F32),
    ]
    queries, cont_q, *state = pl.pallas_call(
        prep_kernel,
        out_shape=[
            shape(((KVH + 1) * HD, rows), BF16),
            shape((KVH * HD, cont_rows), BF16),
        ] + state_shape[:2],
        in_specs=[HBM] * 5,
        out_specs=[VMEM] * 4,
        scratch_shapes=[
            pltpu.SMEM(suffix_length.shape, jnp.int32),
            pltpu.VMEM(new_queries.shape, BF16),
            pltpu.VMEM(cont_queries.shape, BF16),
            pltpu.VMEM(suffix_keys.shape, BF16),
            pltpu.VMEM(suffix_values.shape, BF16),
            pltpu.SemaphoreType.DMA((KVH + 4,)),
        ],
        compiler_params=params,
        cost_estimate=cost(rows, keys),
    )(*[in_hbm(x) for x in (suffix_length, new_queries, cont_queries, suffix_keys, suffix_values)])

    window = pl.pallas_call(
        window_kernel,
        out_shape=shape((2, HD), jnp.int32),
        in_specs=[SMEM] * 2,
        out_specs=VMEM,
        compiler_params=params,
    )(window_start, prefix_length)

    def take(state, held, kind="middle"):
        sources, blocks = zip(*held)
        specs, scratch, outs = [VMEM] * 4, [], state_shape
        if kind == "last":
            outs = [shape(new_queries.shape, BF16), shape(cont_queries.shape, BF16)]
            specs = [HBM] * 2
            scratch = [
                pltpu.VMEM(new_queries.shape, BF16),
                pltpu.VMEM(cont_queries.shape, BF16),
                pltpu.SemaphoreType.DMA((KVH + 1,)),
            ]
        aliases = {} if kind == "last" else {3 + index: index for index in range(len(state))}
        return pl.pallas_call(
            functools.partial(
                take_kernel, size, cache_rows, prompt_rows, cont_count, sources, kind
            ),
            out_shape=outs,
            in_specs=[VMEM] * (3 + len(state) + len(blocks)),
            out_specs=specs,
            scratch_shapes=scratch,
            input_output_aliases=aliases,
            compiler_params=params,
            cost_estimate=cost(rows, len(blocks) * keys),
        )(window, queries, cont_q, *state, *blocks)

    hops = chips // 2
    for hop in range(1, hops):
        own, other = send(own, ring), send(other, ring)
        swap, swop = send(own, pair), send(other, pair)
        state = take(state, waiting, "first" if hop == 1 else "middle")
        arrived = [((hop, False, False), own), ((hop, True, False), swap)]
        waiting = [((hop, False, True), other), ((hop, True, True), swop)]
        if hop + 1 == hops:
            arrived, waiting = arrived + waiting[:1], waiting[1:]
        state = take(state, arrived)
    own = send(own, ring)
    swapped = send(own, pair)
    state = take(state, waiting + [((hops, False, False), own)])
    return tuple(take(state, [((hops, True, False), swapped)], "last"))


def solution(mesh):
    in_specs = (
        P(("grp", "ctx"), None),
        P(("grp", "ctx"), None),
        P(("grp", "ctx"), None),
        P(("grp", "ctx"), None),
        P(("grp", "ctx"), None),
        P(("grp", "ctx"), None),
        P(("grp", "ctx"), None, None),
        P(("grp", "ctx"), None, None),
        P("grp"),
        P("grp"),
        P(("grp", "ctx")),
    )
    out_specs = (P(("grp", "ctx"), None), P(("grp", "ctx"), None))
    size = mesh.shape["ctx"]

    def run(*arrays):
        return body(size, *arrays)

    return jax.shard_map(run, mesh=mesh, in_specs=in_specs, out_specs=out_specs, check_vma=False)
```
